256 devices in a mesh: ctx: 64 (over z, x, core), ch: 4 (over y).
Axes of the slice: x: 4, y: 4, z: 8, core: 2. Of those that a mesh axis runs over, the one named last changes fastest.
Arguments:
- value_in: bfloat16 [256, 131072], P('ch', 'ctx'), may hold values from -6 to 6
- key_gate: bfloat16 [256, 131072], P('ch', 'ctx'), may hold values from -6 to 6
- query_gate: bfloat16 [256, 131072], P('ch', 'ctx'), may hold values from -6 to 6
- filter_taps: float32 [256, 131072], P('ch', 'ctx'), may hold values from -0.015625 to 0.015625
- skip_gain: float32 [256], P('ch'), may hold values from 0.5 to 1.5
- out_weight: bfloat16 [256, 256], P(None, 'ch'), may hold values from -0.375 to 0.375
Outputs:
- mixed_out: bfloat16 [256, 131072], P('ch', 'ctx')
The draws below stay inside these ranges and needn't reach their ends.
All inputs are finite; a program needn't handle non-finite values.
Results may differ from the reference program's by a relative error of at most 0.0049.
Values may be sent and summed in bfloat16 or wider, within the bound.
A program may use at most 64 MiB of HBM per device.

```python
import jax
import jax.numpy as jnp
from jax import lax

CH = 256
TOKENS = 131072


def level_of(rng, shape, shards, smallest, largest):
    gain = 1.0
    for axis_at, parts in shards:
        steps = jax.random.uniform(jax.random.fold_in(jax.random.fold_in(rng, 6), axis_at), (parts,), jnp.float32, smallest / len(shards), largest / len(shards))
        gain = gain * jnp.repeat(jnp.exp(steps), shape[axis_at] // parts).reshape((-1,) + (1,) * (len(shape) - 1 - axis_at))
    return gain


def scatter_about(key, shape, spread, bound, pieces=(), dtype=jnp.bfloat16):
    result = jax.random.normal(key, shape, jnp.float32) * spread
    if len(pieces) > 0:
        result = level_of(key, shape, pieces, -0.22, 0.18) * result
    return jnp.clip(result, min=-bound, max=bound).astype(dtype)


def setup_inputs(seed: int = 0) -> dict:
    arg_keys = jax.random.split(jax.random.key(seed), 7)
    value_in = scatter_about(arg_keys[0], (CH, TOKENS), 1.0, 6.0, ((0, 4), (1, 64)))
    key_gate = scatter_about(arg_keys[1], (CH, TOKENS), 1.0, 6.0, ((0, 4), (1, 64)))
    query_gate = scatter_about(arg_keys[2], (CH, TOKENS), 1.0, 6.0, ((0, 4), (1, 64)))
    filter_taps = scatter_about(arg_keys[3], (CH, TOKENS), TOKENS ** -0.5, 0.015625, ((0, 4), (1, 64)), jnp.float32)
    skip_gain = jnp.clip(0.5 + 1.0 * jax.random.uniform(arg_keys[4], (CH,), jnp.float32) ** level_of(arg_keys[4], (CH,), ((0, 4),), -0.2, 0.2), 0.5, 1.5)
    out_weight = scatter_about(arg_keys[5], (CH, CH), CH ** -0.5, 0.375, ((1, 4),))
    return dict(value_in=value_in, key_gate=key_gate, query_gate=query_gate, filter_taps=filter_taps, skip_gain=skip_gain, out_weight=out_weight)


def reference(value_in, key_gate, query_gate, filter_taps, skip_gain, out_weight):
    signal = value_in.astype(jnp.float32) * key_gate.astype(jnp.float32)
    blocks = CH // 16
    signal_blocks = signal.reshape(blocks, 16, TOKENS)
    taps_blocks = filter_taps.astype(jnp.float32).reshape(blocks, 16, TOKENS)

    def convolve(operands):
        signal_block, taps_block = operands
        spectrum_signal = jnp.fft.rfft(signal_block, n=2 * TOKENS, axis=1)
        spectrum_taps = jnp.fft.rfft(taps_block, n=2 * TOKENS, axis=1)
        return jnp.fft.irfft(spectrum_signal * spectrum_taps, n=2 * TOKENS, axis=1)[:, :TOKENS]

    convolved = lax.map(convolve, (signal_blocks, taps_blocks)).reshape(CH, TOKENS)
    gated_values = (query_gate.astype(jnp.float32) * (convolved + skip_gain[:, None] * value_in.astype(jnp.float32))).astype(jnp.bfloat16)
    mixed_out = jnp.dot(out_weight.T, gated_values, preferred_element_type=jnp.float32)
    return mixed_out.astype(jnp.bfloat16)
```

```python
import functools
import math

import jax
import jax.numpy as jnp
import ml_dtypes
import numpy as np
from jax import lax
from jax.experimental import pallas as pl
from jax.experimental.pallas import tpu as pltpu
from jax.sharding import PartitionSpec as P

F32 = jnp.float32
BF16 = jnp.bfloat16
MESH = pl.DeviceIdType.MESH

N_CTX = 64
N_CH = 4
CHUNK = 2048
ROWS = 16
T = N_CTX * CHUNK
A = 512
B = 256
GROUP = 16
GROUPS = N_CTX // GROUP
TILE = 256


def split(table):
    table = np.asarray(table, np.float32)
    high = table.astype(ml_dtypes.bfloat16)
    return high, (table - high.astype(np.float32)).astype(ml_dtypes.bfloat16)


@functools.cache
def tables():
    freq = np.arange(A)[:, None] + 0.25
    outer = 2 * np.pi * freq * np.arange(A)[None, :] / A
    outer = np.concatenate([np.cos(outer), -np.sin(outer)], 0)
    turn = 2 * np.pi * freq * np.arange(B)[None, :] / T
    inner = 2 * np.pi * np.outer(np.arange(B), np.arange(B)) / B
    c, s = np.cos(inner), np.sin(inner)
    ahead = np.block([[c, -s], [s, c]])
    back = np.block([[c, s], [-s, c]])
    return (
        split(outer),
        split(outer.T / T),
        split(ahead),
        split(back),
        np.cos(turn).astype(np.float32),
        (-np.sin(turn)).astype(np.float32),
    )


def dot(a, b):
    return jnp.dot(a, b, preferred_element_type=F32)


def parts_of(x):
    high = x.astype(BF16)
    return high, (x - high.astype(F32)).astype(BF16)


def times_right(x, table_hi, table_lo):
    high, low = parts_of(x)
    return dot(high, table_hi[...]) + dot(high, table_lo[...]) + dot(low, table_hi[...])


def sub_row(r):
    return (r % 2) * (ROWS // 2) + r // 2


def chunks_to_matrix(recv):
    x = recv[...].astype(F32)
    half = ROWS // 2
    left = x[:, :half, :].reshape(A, 128)
    right = x[:, half:, :].reshape(A, 128)
    return jnp.concatenate([left, right], axis=1).astype(BF16)


def kernel(
    v_hbm, k_hbm, q_hbm, f_hbm, skip_hbm, w_hbm,
    oh_hbm, ol_hbm, ph_hbm, pl_hbm, ah_hbm, al_hbm, bh_hbm, bl_hbm, tc_hbm, ts_hbm,
    out_ref,
    v_ref, k_ref, q_ref, f_ref, skip_row, w_ref,
    oh, ol, ph, plo, ah, al, bh, bl, tc, ts,
    stage, send_s, send_f, send_y, recv_s, recv_f, recv_y,
    skip_ref, x_ref, spec, y_hi, y_lo, conv32, gathered,
    in_sem, table_sem, s_send, s_recv, f_send, f_recv, y_send, y_recv, g_send, g_recv,
):
    me = lax.axis_index("ctx")
    ch = lax.axis_index("ch")

    loads = [
        pltpu.make_async_copy(src, dst, in_sem.at[i])
        for i, (src, dst) in enumerate(
            [(v_hbm, v_ref), (k_hbm, k_ref), (f_hbm, f_ref), (q_hbm, q_ref), (skip_hbm, skip_row), (w_hbm, w_ref)]
        )
    ]
    table_loads = [
        pltpu.make_async_copy(src, dst, table_sem.at[i])
        for i, (src, dst) in enumerate(
            [
                (oh_hbm, oh), (ol_hbm, ol), (tc_hbm, tc), (ts_hbm, ts), (ah_hbm, ah), (al_hbm, al),
                (bh_hbm, bh), (bl_hbm, bl), (ph_hbm, ph), (pl_hbm, plo),
            ]
        )
    ]
    for copy in loads + table_loads:
        copy.start()

    barrier = pltpu.get_barrier_semaphore()

    def greet(o, carry):
        peer = lax.rem(me + o, N_CTX)
        pl.semaphore_signal(barrier, inc=1, device_id=(peer, ch), device_id_type=MESH)
        return carry

    lax.fori_loop(1, N_CTX, greet, 0)
    for o in range(1, N_CH):
        pl.semaphore_signal(barrier, inc=1, device_id=(me, lax.rem(ch + o, N_CH)), device_id_type=MESH)

    def to_chunks(value, send):
        for r in range(ROWS):
            stage[pl.ds(sub_row(r), N_CTX, stride=ROWS), :] = value(r)
        send[...] = stage[...].astype(BF16).reshape(N_CTX, ROWS, 128)

    def tile(ref, r):
        return ref[:, r * 128 : (r + 1) * 128].astype(F32)

    loads[0].wait()
    loads[1].wait()
    to_chunks(lambda r: tile(v_ref, r) * tile(k_ref, r), send_s)
    loads[2].wait()
    to_chunks(lambda r: tile(f_ref, r), send_f)

    pl.semaphore_wait(barrier, N_CTX - 1 + N_CH - 1)

    def chunk_copy(send, recv, s_sem, r_sem, peer):
        return pltpu.make_async_remote_copy(
            src_ref=send.at[peer], dst_ref=recv.at[me], send_sem=s_sem, recv_sem=r_sem,
            device_id=(peer, ch), device_id_type=MESH,
        )

    def scatter(send, recv, s_sem, r_sem):
        pltpu.make_async_copy(send.at[me], recv.at[me], r_sem).start()

        def step(o, carry):
            chunk_copy(send, recv, s_sem, r_sem, lax.rem(me + o, N_CTX)).start()
            return carry

        lax.fori_loop(1, N_CTX, step, 0)

    def whole(ref, s_sem, r_sem):
        return pltpu.make_async_remote_copy(
            src_ref=ref, dst_ref=ref, send_sem=s_sem, recv_sem=r_sem,
            device_id=(lax.rem(me + 1, N_CTX), ch), device_id_type=MESH,
        )

    scatter(send_s, recv_s, s_send, s_recv)
    scatter(send_f, recv_f, f_send, f_recv)

    for copy in table_loads:
        copy.wait()

    def forward(row):
        x = x_ref[...]
        up, down = pl.ds(row, TILE), pl.ds(A + row, TILE)
        re = dot(oh[up, :], x) + dot(ol[up, :], x)
        im = dot(oh[down, :], x) + dot(ol[down, :], x)
        c, s = tc[up, :], ts[up, :]
        return times_right(jnp.concatenate([re * c - im * s, re * s + im * c], axis=1), ah, al)

    whole(recv_s, s_send, s_recv).wait_recv()
    x_ref[...] = chunks_to_matrix(recv_s)

    def signal_step(i, carry):
        row = pl.multiple_of(i * TILE, TILE)
        spec[pl.ds(row, TILE), :] = forward(row)
        return carry

    lax.fori_loop(0, A // TILE, signal_step, 0)

    whole(recv_f, f_send, f_recv).wait_recv()
    x_ref[...] = chunks_to_matrix(recv_f)

    def taps_step(i, carry):
        row = pl.multiple_of(i * TILE, TILE)
        up, down = pl.ds(row, TILE), pl.ds(A + row, TILE)
        taps = forward(row)
        fr, fi = taps[:, :B], taps[:, B:]
        sr, si = spec[up, :B], spec[up, B:]
        product = jnp.concatenate([sr * fr - si * fi, sr * fi + si * fr], axis=1)
        y = times_right(product, bh, bl)
        re, im = y[:, :B], y[:, B:]
        c, s = tc[up, :], ts[up, :]
        re, im = re * c + im * s, im * c - re * s
        y_hi[up, :], y_lo[up, :] = parts_of(re)
        y_hi[down, :], y_lo[down, :] = parts_of(im)
        return carry

    lax.fori_loop(0, A // TILE, taps_step, 0)

    per_group = A // GROUPS
    mine = me // GROUP

    def inverse_step(i, carry):
        g = lax.rem(mine + i, GROUPS)
        rows = pl.ds(pl.multiple_of(g * per_group, per_group), per_group)
        y = dot(ph[rows, :], y_hi[...]) + dot(plo[rows, :], y_hi[...]) + dot(ph[rows, :], y_lo[...])
        half = ROWS // 2
        y = jnp.concatenate(
            [y[:, :128].reshape(GROUP, half, 128), y[:, 128:].reshape(GROUP, half, 128)], axis=1
        )
        send_y[pl.ds(g * GROUP, GROUP)] = y.astype(BF16)

        def step(o, carry):
            peer = g * GROUP + lax.rem(me + o, GROUP)

            @pl.when(peer != me)
            def _():
                chunk_copy(send_y, recv_y, y_send, y_recv.at[mine], peer).start()

            @pl.when(peer == me)
            def _():
                pltpu.make_async_copy(send_y.at[me], recv_y.at[me], y_recv.at[mine]).start()

            return carry

        return lax.fori_loop(0, GROUP, step, carry)

    lax.fori_loop(0, GROUPS, inverse_step, 0)

    for copy in loads[3:]:
        copy.wait()
    eye = lax.broadcasted_iota(jnp.int32, (N_CTX, N_CTX), 0) == lax.broadcasted_iota(jnp.int32, (N_CTX, N_CTX), 1)
    skip_ref[...] = jnp.where(eye, skip_row[...], 0.0)

    def gate_copy(rows, o):
        return pltpu.make_async_remote_copy(
            src_ref=gathered.at[ch, rows], dst_ref=gathered.at[ch, rows],
            send_sem=g_send, recv_sem=g_recv,
            device_id=(me, lax.rem(ch + o, N_CH)), device_id_type=MESH,
        )

    for g in range(GROUPS):
        rows = slice(g * GROUP, (g + 1) * GROUP)
        whole(recv_y.at[rows], y_send, y_recv.at[g]).wait_recv()
        conv32[...] = recv_y[rows].astype(F32).reshape(GROUP * ROWS, 128)
        gain = jnp.sum(skip_ref[rows, :], axis=1, keepdims=True)
        for r in range(ROWS):
            lanes = slice(r * 128, (r + 1) * 128)
            c = conv32[pl.ds(sub_row(r), GROUP, stride=ROWS), :]
            gated = q_ref[rows, lanes].astype(F32) * (c + gain * v_ref[rows, lanes].astype(F32))
            gathered[ch, rows, lanes] = gated.astype(BF16)
        for o in (2, 1, 3):
            gate_copy(pl.ds(g * GROUP, GROUP), o).start()

    three = gathered.at[pl.ds(0, N_CH - 1)]
    done = pltpu.make_async_remote_copy(
        src_ref=three, dst_ref=three, send_sem=g_send, recv_sem=g_recv,
        device_id=(me, lax.rem(ch + 1, N_CH)), device_id_type=MESH,
    )
    done.wait_recv()
    for r in range(CHUNK // 512):
        lanes = slice(r * 512, (r + 1) * 512)
        mixed = lax.dot_general(
            w_ref[...], gathered[:, :, lanes].reshape(N_CH * N_CTX, 512),
            (((0,), (0,)), ((), ())), preferred_element_type=F32,
        )
        out_ref[:, lanes] = mixed.astype(BF16)

    done.wait_send()
    most = pl.ds(0, N_CTX - 1)
    whole(send_s.at[most], s_send, s_recv).wait_send()
    whole(send_f.at[most], f_send, f_recv).wait_send()
    whole(send_y.at[most], y_send, y_recv.at[0]).wait_send()


def on_device(value_in, key_gate, query_gate, filter_taps, skip_gain, out_weight):
    (oh, ol), (ph, plo), (ah, al), (bh, bl), tc, ts = tables()
    consts = [oh, ol, ph, plo, ah, al, bh, bl, tc, ts]
    args = [value_in, key_gate, query_gate, filter_taps, skip_gain.reshape(1, N_CTX), out_weight]
    args += [jnp.asarray(c) for c in consts]
    vm = pltpu.VMEM
    copies = [vm((N_CTX, CHUNK), BF16)] * 3 + [vm((N_CTX, CHUNK), F32), vm((1, N_CTX), F32), vm((N_CH * N_CTX, N_CTX), BF16)]
    copies += [vm(c.shape, c.dtype) for c in consts]
    chunk = vm((N_CTX, ROWS, 128), BF16)
    dma = pltpu.SemaphoreType.DMA
    return pl.pallas_call(
        kernel,
        out_shape=jax.ShapeDtypeStruct((N_CTX, CHUNK), BF16),
        in_specs=[pl.BlockSpec(memory_space=pl.ANY)] * len(args),
        out_specs=pl.BlockSpec(memory_space=pltpu.VMEM),
        scratch_shapes=copies
        + [vm((N_CTX * ROWS, 128), F32)]
        + [chunk] * 6
        + [
            vm((N_CTX, N_CTX), F32),
            vm((A, B), BF16),
            vm((A, 2 * B), F32),
            vm((2 * A, B), BF16),
            vm((2 * A, B), BF16),
            vm((GROUP * ROWS, 128), F32),
            vm((N_CH, N_CTX, CHUNK), BF16),
            dma((6,)), dma((10,)), dma, dma, dma, dma, dma, dma((GROUPS,)), dma, dma,
        ],
        compiler_params=pltpu.CompilerParams(
            collective_id=0, has_side_effects=True, vmem_limit_bytes=48 * 1024 * 1024
        ),
        name="hyena",
    )(*args)


def solution(mesh):
    placed = (
        P("ch", "ctx"),
        P("ch", "ctx"),
        P("ch", "ctx"),
        P("ch", "ctx"),
        P("ch"),
        P(None, "ch"),
    )
    return jax.shard_map(
        on_device, mesh=mesh, in_specs=placed, out_specs=P("ch", "ctx"), check_vma=False
    )
```

```python
import functools

import jax
import jax.numpy as jnp
import numpy as np
from jax import lax
from jax.experimental import pallas as pl
from jax.experimental.pallas import tpu as pltpu
from jax.sharding import PartitionSpec as P

F32 = jnp.float32
BF16 = jnp.bfloat16
MESH = pl.DeviceIdType.MESH

N_CTX = 64
N_CH = 4
CHUNK = 2048
ROWS = 16
T = N_CTX * CHUNK
A = 512
B = 256
GROUP = 16
GROUPS = N_CTX // GROUP
TILE = 256


def turns(rows, columns):
    angle = 2 * np.pi * np.outer(rows, columns)
    return np.stack([np.cos(angle), np.sin(angle)]).astype(np.float32)


@functools.cache
def tables():
    coarse, fine = 16 * np.arange(A // 16), np.arange(16)
    column = np.arange(A)
    return (
        turns(coarse, column / A), turns(fine + 0.25, column / A),
        turns(coarse, (column + 0.25) / A), turns(fine, (column + 0.25) / A),
        turns(coarse[: B // 16], np.arange(B) / B), turns(fine, np.arange(B) / B),
        turns(coarse, np.arange(B) / T), turns(fine + 0.25, np.arange(B) / T),
    )


def dot(a, b):
    return jnp.dot(a, b, preferred_element_type=F32)


def parts_of(x):
    high = x.astype(BF16)
    return high, (x - high.astype(F32)).astype(BF16)


def times_right(x, table_hi, table_lo):
    high, low = parts_of(x)
    return dot(high, table_hi[...]) + dot(high, table_lo[...]) + dot(low, table_hi[...])


def sub_row(r):
    return (r % 2) * (ROWS // 2) + r // 2


def chunks_to_matrix(recv):
    x = recv[...].astype(F32)
    half = ROWS // 2
    left = x[:, :half, :].reshape(A, 128)
    right = x[:, half:, :].reshape(A, 128)
    return jnp.concatenate([left, right], axis=1).astype(BF16)


def kernel(
    v_hbm, k_hbm, q_hbm, f_hbm, skip_hbm, w_hbm,
    fa_hbm, fb_hbm, ga_hbm, gb_hbm, ia_hbm, ib_hbm, ta_hbm, tb_hbm,
    out_ref,
    v_ref, k_ref, q_ref, f_ref, skip_row, w_ref,
    fa, fb, ga, gb, ia, ib, ta, tb,
    oh, ol, ph, plo, ah, al, bh, bl, tc, ts,
    stage, send_s, send_f, send_y, recv_s, recv_f, recv_y,
    skip_ref, x_ref, spec, y_hi, y_lo, conv32, gathered,
    in_sem, table_sem, s_send, s_recv, f_send, f_recv, y_send, y_recv, g_send, g_recv,
):
    me = lax.axis_index("ctx")
    ch = lax.axis_index("ch")

    loads = [
        pltpu.make_async_copy(src, dst, in_sem.at[i])
        for i, (src, dst) in enumerate(
            [(v_hbm, v_ref), (k_hbm, k_ref), (f_hbm, f_ref), (q_hbm, q_ref), (skip_hbm, skip_row), (w_hbm, w_ref)]
        )
    ]
    table_loads = [
        pltpu.make_async_copy(src, dst, table_sem.at[i])
        for i, (src, dst) in enumerate(
            zip(
                (fa_hbm, fb_hbm, ga_hbm, gb_hbm, ia_hbm, ib_hbm, ta_hbm, tb_hbm),
                (fa, fb, ga, gb, ia, ib, ta, tb),
            )
        )
    ]
    for copy in loads + table_loads:
        copy.start()

    barrier = pltpu.get_barrier_semaphore()

    def greet(o, carry):
        peer = lax.rem(me + o, N_CTX)
        pl.semaphore_signal(barrier, inc=1, device_id=(peer, ch), device_id_type=MESH)
        return carry

    lax.fori_loop(1, N_CTX, greet, 0)
    for o in range(1, N_CH):
        pl.semaphore_signal(barrier, inc=1, device_id=(me, lax.rem(ch + o, N_CH)), device_id_type=MESH)

    def to_chunks(value, send):
        for r in range(ROWS):
            stage[pl.ds(sub_row(r), N_CTX, stride=ROWS), :] = value(r)
        send[...] = stage[...].astype(BF16).reshape(N_CTX, ROWS, 128)

    def tile(ref, r):
        return ref[:, r * 128 : (r + 1) * 128].astype(F32)

    loads[0].wait()
    loads[1].wait()
    to_chunks(lambda r: tile(v_ref, r) * tile(k_ref, r), send_s)
    loads[2].wait()
    to_chunks(lambda r: tile(f_ref, r), send_f)

    pl.semaphore_wait(barrier, N_CTX - 1 + N_CH - 1)

    def chunk_copy(send, recv, s_sem, r_sem, peer):
        return pltpu.make_async_remote_copy(
            src_ref=send.at[peer], dst_ref=recv.at[me], send_sem=s_sem, recv_sem=r_sem,
            device_id=(peer, ch), device_id_type=MESH,
        )

    def scatter(send, recv, s_sem, r_sem):
        pltpu.make_async_copy(send.at[me], recv.at[me], r_sem).start()

        def step(o, carry):
            chunk_copy(send, recv, s_sem, r_sem, lax.rem(me + o, N_CTX)).start()
            return carry

        lax.fori_loop(1, N_CTX, step, 0)

    def whole(ref, s_sem, r_sem):
        return pltpu.make_async_remote_copy(
            src_ref=ref, dst_ref=ref, send_sem=s_sem, recv_sem=r_sem,
            device_id=(lax.rem(me + 1, N_CTX), ch), device_id_type=MESH,
        )

    scatter(send_s, recv_s, s_send, s_recv)
    scatter(send_f, recv_f, f_send, f_recv)

    for copy in table_loads:
        copy.wait()

    def block(coarse, fine, i):
        ca, sa = coarse[0, pl.ds(i, 1), :], coarse[1, pl.ds(i, 1), :]
        cb, sb = fine[0], fine[1]
        return ca * cb - sa * sb, ca * sb + sa * cb

    def put(high_ref, low_ref, at, value):
        high_ref[at], low_ref[at] = parts_of(value)

    def make_outer(i, carry):
        up = pl.ds(pl.multiple_of(i * 16, 16), 16)
        down = pl.ds(pl.multiple_of(A + i * 16, 16), 16)
        c, s = block(fa, fb, i)
        put(oh, ol, (up,), c)
        put(oh, ol, (down,), -s)
        c, s = block(ta, tb, i)
        tc[up, :], ts[up, :] = c, -s
        return carry

    def make_inner(i, carry):
        up = pl.ds(pl.multiple_of(i * 16, 16), 16)
        down = pl.ds(pl.multiple_of(B + i * 16, 16), 16)
        left, right = slice(0, B), slice(B, 2 * B)
        c, s = block(ia, ib, i)
        for high, low, sign in ((ah, al, 1.0), (bh, bl, -1.0)):
            put(high, low, (up, left), c)
            put(high, low, (down, right), c)
            put(high, low, (up, right), -sign * s)
            put(high, low, (down, left), sign * s)
        return carry

    def make_last(i, carry):
        up = pl.ds(pl.multiple_of(i * 16, 16), 16)
        c, s = block(ga, gb, i)
        put(ph, plo, (up, slice(0, A)), c * (1.0 / T))
        put(ph, plo, (up, slice(A, 2 * A)), s * (-1.0 / T))
        return carry

    lax.fori_loop(0, A // 16, make_outer, 0)
    lax.fori_loop(0, B // 16, make_inner, 0)
    lax.fori_loop(0, A // 16, make_last, 0)

    def forward(row):
        x = x_ref[...]
        up, down = pl.ds(row, TILE), pl.ds(A + row, TILE)
        re = dot(oh[up, :], x) + dot(ol[up, :], x)
        im = dot(oh[down, :], x) + dot(ol[down, :], x)
        c, s = tc[up, :], ts[up, :]
        return times_right(jnp.concatenate([re * c - im * s, re * s + im * c], axis=1), ah, al)

    whole(recv_s, s_send, s_recv).wait_recv()
    x_ref[...] = chunks_to_matrix(recv_s)

    def signal_step(i, carry):
        row = pl.multiple_of(i * TILE, TILE)
        spec[pl.ds(row, TILE), :] = forward(row)
        return carry

    lax.fori_loop(0, A // TILE, signal_step, 0)

    whole(recv_f, f_send, f_recv).wait_recv()
    x_ref[...] = chunks_to_matrix(recv_f)

    def taps_step(i, carry):
        row = pl.multiple_of(i * TILE, TILE)
        up, down = pl.ds(row, TILE), pl.ds(A + row, TILE)
        taps = forward(row)
        fr, fi = taps[:, :B], taps[:, B:]
        sr, si = spec[up, :B], spec[up, B:]
        product = jnp.concatenate([sr * fr - si * fi, sr * fi + si * fr], axis=1)
        y = times_right(product, bh, bl)
        re, im = y[:, :B], y[:, B:]
        c, s = tc[up, :], ts[up, :]
        re, im = re * c + im * s, im * c - re * s
        y_hi[up, :], y_lo[up, :] = parts_of(re)
        y_hi[down, :], y_lo[down, :] = parts_of(im)
        return carry

    lax.fori_loop(0, A // TILE, taps_step, 0)

    per_group = A // GROUPS
    mine = me // GROUP

    def inverse_step(i, carry):
        g = lax.rem(mine + i, GROUPS)
        rows = pl.ds(pl.multiple_of(g * per_group, per_group), per_group)
        y = dot(ph[rows, :], y_hi[...]) + dot(plo[rows, :], y_hi[...]) + dot(ph[rows, :], y_lo[...])
        half = ROWS // 2
        y = jnp.concatenate(
            [y[:, :128].reshape(GROUP, half, 128), y[:, 128:].reshape(GROUP, half, 128)], axis=1
        )
        send_y[pl.ds(g * GROUP, GROUP)] = y.astype(BF16)

        def step(o, carry):
            peer = g * GROUP + lax.rem(me + o, GROUP)

            @pl.when(peer != me)
            def _():
                chunk_copy(send_y, recv_y, y_send, y_recv.at[mine], peer).start()

            @pl.when(peer == me)
            def _():
                pltpu.make_async_copy(send_y.at[me], recv_y.at[me], y_recv.at[mine]).start()

            return carry

        return lax.fori_loop(0, GROUP, step, carry)

    lax.fori_loop(0, GROUPS, inverse_step, 0)

    for copy in loads[3:]:
        copy.wait()
    eye = lax.broadcasted_iota(jnp.int32, (N_CTX, N_CTX), 0) == lax.broadcasted_iota(jnp.int32, (N_CTX, N_CTX), 1)
    skip_ref[...] = jnp.where(eye, skip_row[...], 0.0)

    def gate_copy(rows, o):
        return pltpu.make_async_remote_copy(
            src_ref=gathered.at[ch, rows], dst_ref=gathered.at[ch, rows],
            send_sem=g_send, recv_sem=g_recv,
            device_id=(me, lax.rem(ch + o, N_CH)), device_id_type=MESH,
        )

    for g in range(GROUPS):
        rows = slice(g * GROUP, (g + 1) * GROUP)
        whole(recv_y.at[rows], y_send, y_recv.at[g]).wait_recv()
        conv32[...] = recv_y[rows].astype(F32).reshape(GROUP * ROWS, 128)
        gain = jnp.sum(skip_ref[rows, :], axis=1, keepdims=True)
        for r in range(ROWS):
            lanes = slice(r * 128, (r + 1) * 128)
            c = conv32[pl.ds(sub_row(r), GROUP, stride=ROWS), :]
            gated = q_ref[rows, lanes].astype(F32) * (c + gain * v_ref[rows, lanes].astype(F32))
            gathered[ch, rows, lanes] = gated.astype(BF16)
        for o in (2, 1, 3):
            gate_copy(pl.ds(g * GROUP, GROUP), o).start()

    three = gathered.at[pl.ds(0, N_CH - 1)]
    done = pltpu.make_async_remote_copy(
        src_ref=three, dst_ref=three, send_sem=g_send, recv_sem=g_recv,
        device_id=(me, lax.rem(ch + 1, N_CH)), device_id_type=MESH,
    )
    done.wait_recv()
    for r in range(CHUNK // 512):
        lanes = slice(r * 512, (r + 1) * 512)
        mixed = dot(w_ref[...], gathered[:, :, lanes].reshape(N_CH * N_CTX, 512))
        out_ref[:, lanes] = mixed.astype(BF16)

    done.wait_send()
    most = pl.ds(0, N_CTX - 1)
    whole(send_s.at[most], s_send, s_recv).wait_send()
    whole(send_f.at[most], f_send, f_recv).wait_send()
    whole(send_y.at[most], y_send, y_recv.at[0]).wait_send()


def on_device(value_in, key_gate, query_gate, filter_taps, skip_gain, out_weight):
    consts = tables()
    args = [value_in, key_gate, query_gate, filter_taps, skip_gain.reshape(1, N_CTX), out_weight.T]
    args += [jnp.asarray(c) for c in consts]
    vm = pltpu.VMEM
    copies = [vm((N_CTX, CHUNK), BF16)] * 3 + [vm((N_CTX, CHUNK), F32), vm((1, N_CTX), F32), vm((N_CTX, N_CH * N_CTX), BF16)]
    copies += [vm(c.shape, c.dtype) for c in consts]
    copies += [vm((2 * A, A), BF16)] * 2 + [vm((A, 2 * A), BF16)] * 2 + [vm((2 * B, 2 * B), BF16)] * 4 + [vm((A, B), F32)] * 2
    chunk = vm((N_CTX, ROWS, 128), BF16)
    dma = pltpu.SemaphoreType.DMA
    return pl.pallas_call(
        kernel,
        out_shape=jax.ShapeDtypeStruct((N_CTX, CHUNK), BF16),
        in_specs=[pl.BlockSpec(memory_space=pltpu.HBM)] * len(args),
        out_specs=pl.BlockSpec(memory_space=pltpu.VMEM),
        scratch_shapes=copies
        + [vm((N_CTX * ROWS, 128), F32)]
        + [chunk] * 6
        + [
            vm((N_CTX, N_CTX), F32),
            vm((A, B), BF16),
            vm((A, 2 * B), F32),
            vm((2 * A, B), BF16),
            vm((2 * A, B), BF16),
            vm((GROUP * ROWS, 128), F32),
            vm((N_CH, N_CTX, CHUNK), BF16),
            dma((6,)), dma((8,)), dma, dma, dma, dma, dma, dma((GROUPS,)), dma, dma,
        ],
        compiler_params=pltpu.CompilerParams(
            collective_id=0, has_side_effects=True, vmem_limit_bytes=56 * 1024 * 1024
        ),
        name="hyena",
    )(*args)


def solution(mesh):
    placed = (
        P("ch", "ctx"),
        P("ch", "ctx"),
        P("ch", "ctx"),
        P("ch", "ctx"),
        P("ch"),
        P(None, "ch"),
    )
    return jax.shard_map(
        on_device, mesh=mesh, in_specs=placed, out_specs=P("ch", "ctx"), check_vma=False
    )
```

```python
import functools

import jax
import jax.numpy as jnp
import numpy as np
from jax import lax
from jax.experimental import pallas as pl
from jax.experimental.pallas import tpu as pltpu
from jax.sharding import PartitionSpec as P

F32 = jnp.float32
BF16 = jnp.bfloat16
MESH = pl.DeviceIdType.MESH

N_CTX = 64
N_CH = 4
CHUNK = 2048
ROWS = 16
T = N_CTX * CHUNK
A = 512
B = 256
GROUP = 16
GROUPS = N_CTX // GROUP
PIECES = ROWS // N_CH
TILE = 256


def turns(rows, columns):
    angle = 2 * np.pi * np.outer(rows, columns)
    return np.stack([np.cos(angle), np.sin(angle)]).astype(np.float32)


@functools.cache
def tables():
    coarse, fine = 16 * np.arange(A // 16), np.arange(16)
    column = np.arange(A)
    return (
        turns(coarse, column / A), turns(fine + 0.25, column / A),
        turns(coarse, (column + 0.25) / A), turns(fine, (column + 0.25) / A),
        turns(coarse[: B // 16], np.arange(B) / B), turns(fine, np.arange(B) / B),
        turns(coarse, np.arange(B) / T), turns(fine + 0.25, np.arange(B) / T),
    )


def dot(a, b):
    return jnp.dot(a, b, preferred_element_type=F32)


def parts_of(x):
    high = x.astype(BF16)
    return high, (x - high.astype(F32)).astype(BF16)


def times_right(x, table_hi, table_lo):
    high, low = parts_of(x)
    return dot(high, table_hi[...]) + dot(high, table_lo[...]) + dot(low, table_hi[...])


def sub_row(r):
    return (r % 2) * (ROWS // 2) + r // 2


def lane_tile(y, i):
    return 8 * (y % 2) + 2 * i + y // 2


def chunks_to_matrix(recv):
    x = recv[...].astype(F32)
    half = ROWS // 2
    left = x[:, :half, :].reshape(A, 128)
    right = x[:, half:, :].reshape(A, 128)
    return jnp.concatenate([left, right], axis=1).astype(BF16)


def kernel(
    v_hbm, k_hbm, q_hbm, f_hbm, skip_hbm, w_hbm,
    fa_hbm, fb_hbm, ga_hbm, gb_hbm, ia_hbm, ib_hbm, ta_hbm, tb_hbm,
    out_ref,
    v_ref, k_ref, q_ref, f_ref, skip_row, w_ref, skip_all, w_all,
    fa, fb, ga, gb, ia, ib, ta, tb,
    oh, ol, ph, plo, ah, al, bh, bl, tc, ts,
    stage, send_s, send_f, send_y, recv_s, recv_f, recv_y,
    side_out, side_in, gain_v, x_ref, spec, y_hi, y_lo, conv32, gated, mix_out, mix_in,
    in_sem, table_sem, s_send, s_recv, f_send, f_recv, y_send, y_recv, side_send, side_recv, small_send, small_recv,
    mix_send, mix_recv, ready,
):
    me = lax.axis_index("ctx")
    ch = lax.axis_index("ch")

    loads = [
        pltpu.make_async_copy(src, dst, in_sem.at[i])
        for i, (src, dst) in enumerate(
            [(v_hbm, v_ref), (k_hbm, k_ref), (f_hbm, f_ref), (q_hbm, q_ref), (skip_hbm, skip_row), (w_hbm, w_ref)]
        )
    ]
    table_loads = [
        pltpu.make_async_copy(src, dst, table_sem.at[i])
        for i, (src, dst) in enumerate(
            zip(
                (fa_hbm, fb_hbm, ga_hbm, gb_hbm, ia_hbm, ib_hbm, ta_hbm, tb_hbm),
                (fa, fb, ga, gb, ia, ib, ta, tb),
            )
        )
    ]
    for copy in loads + table_loads:
        copy.start()

    barrier = pltpu.get_barrier_semaphore()

    def greet(o, carry):
        peer = lax.rem(me + o, N_CTX)
        pl.semaphore_signal(barrier, inc=1, device_id=(peer, ch), device_id_type=MESH)
        return carry

    lax.fori_loop(1, N_CTX, greet, 0)
    for o in range(1, N_CH):
        pl.semaphore_signal(barrier, inc=1, device_id=(me, lax.rem(ch + o, N_CH)), device_id_type=MESH)

    def to_chunks(value, send):
        for r in range(ROWS):
            stage[pl.ds(sub_row(r), N_CTX, stride=ROWS), :] = value(r)
        send[...] = stage[...].astype(BF16).reshape(N_CTX, ROWS, 128)

    def tile(ref, r):
        return ref[:, r * 128 : (r + 1) * 128].astype(F32)

    loads[0].wait()
    loads[1].wait()
    to_chunks(lambda r: tile(v_ref, r) * tile(k_ref, r), send_s)
    loads[2].wait()
    to_chunks(lambda r: tile(f_ref, r), send_f)

    pl.semaphore_wait(barrier, N_CTX - 1 + N_CH - 1)
    for o in range(1, N_CH):
        pl.semaphore_signal(ready, inc=1, device_id=(me, lax.rem(ch + o, N_CH)), device_id_type=MESH)

    def chunk_copy(send, recv, s_sem, r_sem, peer):
        return pltpu.make_async_remote_copy(
            src_ref=send.at[peer], dst_ref=recv.at[me], send_sem=s_sem, recv_sem=r_sem,
            device_id=(peer, ch), device_id_type=MESH,
        )

    def far_first(i):
        j = i - 8
        reach = 3 - j // 16
        dz = jnp.where(j % 2 == 0, reach, 8 - reach)
        inner = j % 16 // 2
        dz, inner = jnp.where(i < 8, 4, dz), jnp.where(i < 8, i, inner)
        dz, inner = jnp.where(i < 56, dz, 0), jnp.where(i < 56, inner, i - 55)
        z, x, core = me // 8, me % 8 // 2, me % 2
        z, x, core = (z + dz) % 8, (x + inner // 2) % 4, (core + inner) % 2
        return z * 8 + x * 2 + core

    def scatter(send, recv, s_sem, r_sem):
        pltpu.make_async_copy(send.at[me], recv.at[me], r_sem).start()

        def step(i, carry):
            chunk_copy(send, recv, s_sem, r_sem, far_first(i)).start()
            return carry

        lax.fori_loop(0, N_CTX - 1, step, 0)

    def whole(ref, s_sem, r_sem):
        return pltpu.make_async_remote_copy(
            src_ref=ref, dst_ref=ref, send_sem=s_sem, recv_sem=r_sem,
            device_id=(lax.rem(me + 1, N_CTX), ch), device_id_type=MESH,
        )

    scatter(send_s, recv_s, s_send, s_recv)
    scatter(send_f, recv_f, f_send, f_recv)

    def to_peer(src, dst, s_sem, r_sem, o):
        return pltpu.make_async_remote_copy(
            src_ref=src, dst_ref=dst, send_sem=s_sem, recv_sem=r_sem,
            device_id=(me, lax.rem(ch + o, N_CH)), device_id_type=MESH,
        )

    for copy in loads[3:]:
        copy.wait()
    for y in range(N_CH):
        for i in range(PIECES):
            src = slice(lane_tile(y, i) * 128, lane_tile(y, i) * 128 + 128)
            dst = slice(i * 128, i * 128 + 128)
            side_out[y, 0, :, dst] = q_ref[:, src]
            side_out[y, 1, :, dst] = v_ref[:, src]
    pl.semaphore_wait(ready, N_CH - 1)
    for o in (2, 1, 3):
        to_peer(skip_row, skip_all.at[ch], small_send.at[0], small_recv.at[0], o).start()
        to_peer(w_ref, w_all.at[ch], small_send.at[1], small_recv.at[1], o).start()
        to_peer(side_out.at[lax.rem(ch + o, N_CH)], side_in.at[ch], side_send, side_recv, o).start()
    skip_all[ch] = skip_row[...]
    w_all[ch] = w_ref[...]
    side_in[ch] = side_out[ch]

    for copy in table_loads:
        copy.wait()

    def block(coarse, fine, i):
        ca, sa = coarse[0, pl.ds(i, 1), :], coarse[1, pl.ds(i, 1), :]
        cb, sb = fine[0], fine[1]
        return ca * cb - sa * sb, ca * sb + sa * cb

    def put(high_ref, low_ref, at, value):
        high_ref[at], low_ref[at] = parts_of(value)

    def make_outer(i, carry):
        up = pl.ds(pl.multiple_of(i * 16, 16), 16)
        down = pl.ds(pl.multiple_of(A + i * 16, 16), 16)
        c, s = block(fa, fb, i)
        put(oh, ol, (up,), c)
        put(oh, ol, (down,), -s)
        c, s = block(ta, tb, i)
        tc[up, :], ts[up, :] = c, -s
        return carry

    def make_inner(i, carry):
        up = pl.ds(pl.multiple_of(i * 16, 16), 16)
        down = pl.ds(pl.multiple_of(B + i * 16, 16), 16)
        left, right = slice(0, B), slice(B, 2 * B)
        c, s = block(ia, ib, i)
        for high, low, sign in ((ah, al, 1.0), (bh, bl, -1.0)):
            put(high, low, (up, left), c)
            put(high, low, (down, right), c)
            put(high, low, (up, right), -sign * s)
            put(high, low, (down, left), sign * s)
        return carry

    def make_last(i, carry):
        up = pl.ds(pl.multiple_of(i * 16, 16), 16)
        c, s = block(ga, gb, i)
        put(ph, plo, (up, slice(0, A)), c * (1.0 / T))
        put(ph, plo, (up, slice(A, 2 * A)), s * (-1.0 / T))
        return carry

    lax.fori_loop(0, A // 16, make_outer, 0)
    lax.fori_loop(0, B // 16, make_inner, 0)
    lax.fori_loop(0, A // 16, make_last, 0)

    def forward(row):
        x = x_ref[...]
        up, down = pl.ds(row, TILE), pl.ds(A + row, TILE)
        re = dot(oh[up, :], x) + dot(ol[up, :], x)
        im = dot(oh[down, :], x) + dot(ol[down, :], x)
        c, s = tc[up, :], ts[up, :]
        return times_right(jnp.concatenate([re * c - im * s, re * s + im * c], axis=1), ah, al)

    whole(recv_s, s_send, s_recv).wait_recv()
    x_ref[...] = chunks_to_matrix(recv_s)

    def signal_step(i, carry):
        row = pl.multiple_of(i * TILE, TILE)
        spec[pl.ds(row, TILE), :] = forward(row)
        return carry

    lax.fori_loop(0, A // TILE, signal_step, 0)

    whole(recv_f, f_send, f_recv).wait_recv()
    x_ref[...] = chunks_to_matrix(recv_f)

    def taps_step(i, carry):
        row = pl.multiple_of(i * TILE, TILE)
        up, down = pl.ds(row, TILE), pl.ds(A + row, TILE)
        taps = forward(row)
        fr, fi = taps[:, :B], taps[:, B:]
        sr, si = spec[up, :B], spec[up, B:]
        product = jnp.concatenate([sr * fr - si * fi, sr * fi + si * fr], axis=1)
        y = times_right(product, bh, bl)
        re, im = y[:, :B], y[:, B:]
        c, s = tc[up, :], ts[up, :]
        re, im = re * c + im * s, im * c - re * s
        y_hi[up, :], y_lo[up, :] = parts_of(re)
        y_hi[down, :], y_lo[down, :] = parts_of(im)
        return carry

    lax.fori_loop(0, A // TILE, taps_step, 0)

    per_group = A // GROUPS
    mine = me // GROUP

    def group_at(i):
        return jnp.where(i < 2, 2 - i, 9 - 3 * i)

    def inverse_step(i, carry):
        g = lax.rem(mine + group_at(i), GROUPS)
        rows = pl.ds(pl.multiple_of(g * per_group, per_group), per_group)
        y = dot(ph[rows, :], y_hi[...]) + dot(plo[rows, :], y_hi[...]) + dot(ph[rows, :], y_lo[...])
        for h in range(2):
            part = y[:, h * 128 : h * 128 + 128].reshape(GROUP, 2, PIECES, 128).astype(BF16)
            for p in range(2):
                send_y[h * 2 + p, pl.ds(g * GROUP, GROUP)] = part[:, p]

        def step(o, carry):
            peer = g * GROUP + lax.rem(me + o // N_CH, GROUP)
            to = lax.rem(ch + o, N_CH)
            own = jnp.logical_and(peer == me, to == ch)

            @pl.when(jnp.logical_not(own))
            def _():
                pltpu.make_async_remote_copy(
                    src_ref=send_y.at[to, peer], dst_ref=recv_y.at[ch, me],
                    send_sem=y_send, recv_sem=y_recv.at[ch],
                    device_id=(peer, to), device_id_type=MESH,
                ).start()

            @pl.when(own)
            def _():
                pltpu.make_async_copy(send_y.at[to, peer], recv_y.at[ch, me], y_recv.at[ch]).start()

            return carry

        return lax.fori_loop(0, GROUP * N_CH, step, carry)

    lax.fori_loop(0, GROUPS, inverse_step, 0)

    three = pl.ds(0, N_CH - 1)
    to_peer(skip_all.at[three], skip_all.at[three], small_send.at[0], small_recv.at[0], 1).wait_recv()
    to_peer(w_all.at[three], w_all.at[three], small_send.at[1], small_recv.at[1], 1).wait_recv()
    to_peer(side_in.at[three], side_in.at[three], side_send, side_recv, 1).wait_recv()
    eye = lax.broadcasted_iota(jnp.int32, (N_CTX, N_CTX), 0) == lax.broadcasted_iota(jnp.int32, (N_CTX, N_CTX), 1)
    for y in range(N_CH):
        gain = jnp.sum(jnp.where(eye, skip_all[y], 0.0), axis=1, keepdims=True)
        gain_v[y] = gain * side_in[y, 1].astype(F32)

    for y in range(N_CH):
        whole(recv_y.at[y], y_send, y_recv.at[y]).wait_recv()
        conv32[...] = recv_y[y].astype(F32).reshape(N_CTX * PIECES, 128)
        for i in range(PIECES):
            lanes = slice(i * 128, i * 128 + 128)
            c = conv32[pl.ds(i, N_CTX, stride=PIECES), :]
            value = side_in[y, 0, :, lanes].astype(F32) * (c + gain_v[y, :, lanes])
            gated[y * N_CTX : (y + 1) * N_CTX, lanes] = value.astype(BF16)

    mixed = dot(w_all[...].reshape(N_CH * N_CTX, N_CH * N_CTX), gated[...])
    mix_out[...] = mixed.astype(BF16).reshape(N_CH, N_CTX, PIECES * 128)
    for o in (2, 1, 3):
        to_peer(mix_out.at[lax.rem(ch + o, N_CH)], mix_in.at[ch], mix_send, mix_recv, o).start()
    mix_in[ch] = mix_out[ch]
    to_peer(mix_in.at[three], mix_in.at[three], mix_send, mix_recv, 1).wait_recv()
    for y in range(N_CH):
        for i in range(PIECES):
            at = lane_tile(y, i) * 128
            out_ref[:, at : at + 128] = mix_in[y, :, i * 128 : i * 128 + 128]

    to_peer(skip_all.at[three], skip_all.at[three], small_send.at[0], small_recv.at[0], 1).wait_send()
    to_peer(w_all.at[three], w_all.at[three], small_send.at[1], small_recv.at[1], 1).wait_send()
    to_peer(side_in.at[three], side_in.at[three], side_send, side_recv, 1).wait_send()
    to_peer(mix_in.at[three], mix_in.at[three], mix_send, mix_recv, 1).wait_send()
    most = pl.ds(0, N_CTX - 1)
    whole(send_s.at[most], s_send, s_recv).wait_send()
    whole(send_f.at[most], f_send, f_recv).wait_send()
    whole(send_y.at[three], y_send, y_recv.at[0]).wait_send()
    whole(send_y.at[0, most], y_send, y_recv.at[0]).wait_send()


def on_device(value_in, key_gate, query_gate, filter_taps, skip_gain, out_weight):
    consts = tables()
    args = [value_in, key_gate, query_gate, filter_taps, skip_gain.reshape(1, N_CTX), out_weight.T]
    args += [jnp.asarray(c) for c in consts]
    vm = pltpu.VMEM
    copies = [vm((N_CTX, CHUNK), BF16)] * 3 + [vm((N_CTX, CHUNK), F32), vm((1, N_CTX), F32), vm((N_CTX, N_CH * N_CTX), BF16)]
    copies += [vm((N_CH, 1, N_CTX), F32), vm((N_CH, N_CTX, N_CH * N_CTX), BF16)]
    copies += [vm(c.shape, c.dtype) for c in consts]
    copies += [vm((2 * A, A), BF16)] * 2 + [vm((A, 2 * A), BF16)] * 2 + [vm((2 * B, 2 * B), BF16)] * 4 + [vm((A, B), F32)] * 2
    chunk = vm((N_CTX, ROWS, 128), BF16)
    dma = pltpu.SemaphoreType.DMA
    return pl.pallas_call(
        kernel,
        out_shape=jax.ShapeDtypeStruct((N_CTX, CHUNK), BF16),
        in_specs=[pl.BlockSpec(memory_space=pltpu.HBM)] * len(args),
        out_specs=pl.BlockSpec(memory_space=pltpu.VMEM),
        scratch_shapes=copies
        + [vm((N_CTX * ROWS, 128), F32)]
        + [chunk] * 2
        + [vm((N_CH, N_CTX, PIECES, 128), BF16)]
        + [chunk] * 2
        + [vm((N_CH, N_CTX, PIECES, 128), BF16)]
        + [vm((N_CH, 2, N_CTX, CHUNK // N_CH), BF16)] * 2
        + [
            vm((N_CH, N_CTX, CHUNK // N_CH), F32),
            vm((A, B), BF16),
            vm((A, 2 * B), F32),
            vm((2 * A, B), BF16),
            vm((2 * A, B), BF16),
            vm((N_CTX * PIECES, 128), F32),
            vm((N_CH * N_CTX, CHUNK // N_CH), BF16),
            vm((N_CH, N_CTX, CHUNK // N_CH), BF16),
            vm((N_CH, N_CTX, CHUNK // N_CH), BF16),
            dma((6,)), dma((8,)), dma, dma, dma, dma, dma, dma((N_CH,)), dma, dma, dma((2,)), dma((2,)),
            dma, dma, pltpu.SemaphoreType.REGULAR,
        ],
        compiler_params=pltpu.CompilerParams(
            collective_id=0, has_side_effects=True, vmem_limit_bytes=56 * 1024 * 1024
        ),
        name="hyena",
    )(*args)


def solution(mesh):
    placed = (
        P("ch", "ctx"),
        P("ch", "ctx"),
        P("ch", "ctx"),
        P("ch", "ctx"),
        P("ch"),
        P(None, "ch"),
    )
    return jax.shard_map(
        on_device, mesh=mesh, in_specs=placed, out_specs=P("ch", "ctx"), check_vma=False
    )
```

```python
import functools

import jax
import jax.numpy as jnp
import numpy as np
from jax import lax
from jax.experimental import pallas as pl
from jax.experimental.pallas import tpu as pltpu
from jax.sharding import PartitionSpec as P

F32 = jnp.float32
BF16 = jnp.bfloat16
MESH = pl.DeviceIdType.MESH

N_CTX = 64
N_CH = 4
CHUNK = 2048
ROWS = 16
T = N_CTX * CHUNK
A = 256
B = 512
PIECES = ROWS // N_CH
TILE = 32


def turns(rows, columns):
    angle = 2 * np.pi * np.outer(rows, columns)
    return np.stack([np.cos(angle), np.sin(angle)]).astype(np.float32)


@functools.cache
def tables():
    coarse, fine = 16 * np.arange(A // 16), np.arange(16)
    freq, column = np.arange(A) + 0.25, np.arange(B)
    inner = (4 * np.arange(128)[None, :] + np.arange(4)[:, None]).reshape(-1) / B
    lanes = np.tile(np.arange(128), 4)
    back = turns(fine, 4 * lanes / B)
    shift = np.repeat(np.arange(4), 128) * lanes / B
    cs, sn = np.cos(2 * np.pi * shift), np.sin(2 * np.pi * shift)
    back = np.stack([back[0] * cs - back[1] * sn, back[1] * cs + back[0] * sn]).astype(np.float32)
    return (
        turns(coarse, np.arange(A) / A), turns(fine + 0.25, np.arange(A) / A),
        turns(coarse, freq / A), turns(fine, freq / A),
        turns(coarse[:8], inner), turns(fine, inner),
        turns(coarse[:8], 4 * lanes / B), back,
        turns(coarse, column / T), turns(fine + 0.25, column / T),
    )


def dot(a, b):
    return jnp.dot(a, b, preferred_element_type=F32)


def parts_of(x):
    high = x.astype(BF16)
    return high, (x - high.astype(F32)).astype(BF16)


def lane_tile(y, i):
    return 4 * i + y


def mul(a, b):
    return a[0] * b[0] - a[1] * b[1], a[0] * b[1] + a[1] * b[0]


def mul_conj(a, b):
    return a[0] * b[0] + a[1] * b[1], a[1] * b[0] - a[0] * b[1]


def add(a, b):
    return a[0] + b[0], a[1] + b[1]


def sub(a, b):
    return a[0] - b[0], a[1] - b[1]


def four_point(x, sign):
    even, odd = add(x[0], x[2]), add(x[1], x[3])
    even_d, odd_d = sub(x[0], x[2]), sub(x[1], x[3])
    turned = (-sign * odd_d[1], sign * odd_d[0])
    return add(even, odd), add(even_d, turned), sub(even, odd), sub(even_d, turned)


def kernel(
    v_hbm, k_hbm, q_hbm, f_hbm, skip_hbm, w_hbm,
    fa_hbm, fb_hbm, ga_hbm, gb_hbm, ia_hbm, ib_hbm, ja_hbm, jb_hbm, ta_hbm, tb_hbm,
    out_ref,
    v_ref, k_ref, q_ref, f_ref, skip_row, w_ref, skip_all, w_all,
    fa, fb, ga, gb, ia, ib, ja, jb, ta, tb,
    oh, ol, ph, plo, ah, al, bh, bl, tc, ts,
    stage, send_s, send_f, send_y, recv_s, recv_f, recv_y,
    side_out, side_in, gain_v, x_ref, z_ref, s_hi, s_lo, spec, f_spec, y_hi, y_lo, conv32, gated, mix_out, mix_in,
    in_sem, table_sem, s_send, s_recv, f_send, f_recv, y_send, y_recv, side_send, side_recv, small_send, small_recv,
    mix_send, mix_recv, ready,
):
    me = lax.axis_index("ctx")
    ch = lax.axis_index("ch")

    loads = [
        pltpu.make_async_copy(src, dst, in_sem.at[i])
        for i, (src, dst) in enumerate(
            [(v_hbm, v_ref), (k_hbm, k_ref), (f_hbm, f_ref), (q_hbm, q_ref), (skip_hbm, skip_row), (w_hbm, w_ref)]
        )
    ]
    table_loads = [
        pltpu.make_async_copy(src, dst, table_sem.at[i])
        for i, (src, dst) in enumerate(
            zip(
                (fa_hbm, fb_hbm, ga_hbm, gb_hbm, ia_hbm, ib_hbm, ja_hbm, jb_hbm, ta_hbm, tb_hbm),
                (fa, fb, ga, gb, ia, ib, ja, jb, ta, tb),
            )
        )
    ]
    for copy in loads + table_loads:
        copy.start()

    barrier = pltpu.get_barrier_semaphore()

    def wrap(value, size):
        return jnp.where(value >= size, value - size, value)

    def greet(o, carry):
        pl.semaphore_signal(barrier, inc=1, device_id=(wrap(me + o, N_CTX), ch), device_id_type=MESH)
        return carry

    lax.fori_loop(1, N_CTX, greet, 0, unroll=3)
    for o in range(1, N_CH):
        pl.semaphore_signal(barrier, inc=1, device_id=(me, lax.rem(ch + o, N_CH)), device_id_type=MESH)

    def to_chunks(value, send):
        for r in range(ROWS):
            stage[pl.ds(r, N_CTX, stride=ROWS), :] = value(r)
        send[...] = stage[...].astype(BF16).reshape(N_CTX, ROWS, 128)

    def tile(ref, r):
        return ref[:, r * 128 : (r + 1) * 128].astype(F32)

    loads[0].wait()
    loads[1].wait()
    to_chunks(lambda r: tile(v_ref, r) * tile(k_ref, r), send_s)
    loads[2].wait()
    to_chunks(lambda r: tile(f_ref, r), send_f)

    pl.semaphore_wait(barrier, N_CTX - 1 + N_CH - 1)
    for o in range(1, N_CH):
        pl.semaphore_signal(ready, inc=1, device_id=(me, lax.rem(ch + o, N_CH)), device_id_type=MESH)

    def chunk_copy(send, recv, s_sem, r_sem, peer):
        return pltpu.make_async_remote_copy(
            src_ref=send.at[peer], dst_ref=recv.at[me], send_sem=s_sem, recv_sem=r_sem,
            device_id=(peer, ch), device_id_type=MESH,
        )

    z, lane = me // 8, me % 8

    def scatter(send, recv, s_sem, r_sem):
        for offsets in ((4,), (3, 5), (2, 6), (1, 7)):
            bases = [wrap(z + dz, 8) * 8 for dz in offsets]

            def step(i, carry, bases=bases):
                to = wrap(lane + i, 8)
                for base in bases:
                    chunk_copy(send, recv, s_sem, r_sem, base + to).start()
                return carry

            lax.fori_loop(0, 8, step, 0, unroll=2)

        def near(i, carry):
            chunk_copy(send, recv, s_sem, r_sem, z * 8 + wrap(lane + i, 8)).start()
            return carry

        lax.fori_loop(1, 8, near, 0)
        pltpu.make_async_copy(send.at[me], recv.at[me], r_sem).start()

    def whole(ref, s_sem, r_sem):
        return pltpu.make_async_remote_copy(
            src_ref=ref, dst_ref=ref, send_sem=s_sem, recv_sem=r_sem,
            device_id=(lax.rem(me + 1, N_CTX), ch), device_id_type=MESH,
        )

    scatter(send_s, recv_s, s_send, s_recv)
    scatter(send_f, recv_f, f_send, f_recv)

    def to_peer(src, dst, s_sem, r_sem, o):
        return pltpu.make_async_remote_copy(
            src_ref=src, dst_ref=dst, send_sem=s_sem, recv_sem=r_sem,
            device_id=(me, lax.rem(ch + o, N_CH)), device_id_type=MESH,
        )

    for copy in loads[3:]:
        copy.wait()
    for y in range(N_CH):
        for i in range(PIECES):
            src = slice(lane_tile(y, i) * 128, lane_tile(y, i) * 128 + 128)
            dst = slice(i * 128, i * 128 + 128)
            side_out[y, 0, :, dst] = q_ref[:, src]
            side_out[y, 1, :, dst] = v_ref[:, src]
    pl.semaphore_wait(ready, N_CH - 1)
    for o in (2, 1, 3):
        to_peer(skip_row, skip_all.at[ch], small_send.at[0], small_recv.at[0], o).start()
        to_peer(w_ref, w_all.at[ch], small_send.at[1], small_recv.at[1], o).start()
        to_peer(side_out.at[lax.rem(ch + o, N_CH)], side_in.at[ch], side_send, side_recv, o).start()
    skip_all[ch] = skip_row[...]
    w_all[ch] = w_ref[...]
    side_in[ch] = side_out[ch]

    for copy in table_loads:
        copy.wait()

    def block(coarse, fine, i):
        ca, sa = coarse[0, pl.ds(i, 1), :], coarse[1, pl.ds(i, 1), :]
        cb, sb = fine[0], fine[1]
        return ca * cb - sa * sb, ca * sb + sa * cb

    def put(high_ref, low_ref, at, value):
        high_ref[at], low_ref[at] = parts_of(value)

    def make_outer(i, carry):
        up = pl.ds(pl.multiple_of(i * 16, 16), 16)
        down = pl.ds(pl.multiple_of(A + i * 16, 16), 16)
        c, s = block(fa, fb, i)
        put(oh, ol, (up,), c)
        put(oh, ol, (down,), -s)
        c, s = block(ga, gb, i)
        put(ph, plo, (up, slice(0, A)), c * (1.0 / T))
        put(ph, plo, (up, slice(A, 2 * A)), s * (-1.0 / T))
        c, s = block(ta, tb, i)
        tc[up, :], ts[up, :] = c, -s
        return carry

    def make_inner(i, carry):
        up = pl.ds(pl.multiple_of(i * 16, 16), 16)
        down = pl.ds(pl.multiple_of(128 + i * 16, 16), 16)
        left, right = slice(0, 128), slice(128, 256)
        for high, low, coarse, fine, sign in ((ah, al, ia, ib, 1.0), (bh, bl, ja, jb, -1.0)):
            c, s = block(coarse, fine, i)
            for k in range(4):
                ck, sk = c[:, k * 128 : k * 128 + 128], s[:, k * 128 : k * 128 + 128]
                put(high, low, (k, up, left), ck)
                put(high, low, (k, down, right), ck)
                put(high, low, (k, up, right), -sign * sk)
                put(high, low, (k, down, left), sign * sk)
        return carry

    lax.fori_loop(0, A // 16, make_outer, 0)
    lax.fori_loop(0, 8, make_inner, 0)

    def load_matrix(recv):
        stage[...] = recv[...].astype(F32).reshape(N_CTX * ROWS, 128)
        for r in range(4):
            x_ref[:, r * 128 : r * 128 + 128] = stage[pl.ds(r, A, stride=4), :].astype(BF16)

    def pair(ref, rows, k, imag):
        return ref[rows, k * 128 : k * 128 + 128], ref[imag, k * 128 : k * 128 + 128]

    def put_pair(k, rows, value):
        for part, at in ((value[0], k * 256), (value[1], k * 256 + 128)):
            s_hi[rows, at : at + 128], s_lo[rows, at : at + 128] = parts_of(part)

    def inner(high, low, k):
        at = slice(k * 256, k * 256 + 256)
        return dot(s_hi[:, at], high[k]) + dot(s_hi[:, at], low[k]) + dot(s_lo[:, at], high[k])

    def forward(recv, out):
        load_matrix(recv)
        z_ref[...] = dot(oh[...], x_ref[...]) + dot(ol[...], x_ref[...])
        for row in range(0, A, TILE):
            rows, imag = slice(row, row + TILE), slice(A + row, A + row + TILE)
            turned = []
            for r in range(4):
                at = slice(r * 128, r * 128 + 128)
                turned.append(mul(pair(z_ref, rows, r, imag), (tc[rows, at], ts[rows, at])))
            for k, value in enumerate(four_point(turned, -1.0)):
                put_pair(k, rows, value)
        for k in range(4):
            out[:, k * 256 : k * 256 + 256] = inner(ah, al, k)

    whole(recv_s, s_send, s_recv).wait_recv()
    forward(recv_s, spec)

    whole(recv_f, f_send, f_recv).wait_recv()
    forward(recv_f, f_spec)
    for k in range(4):
        at, half = slice(k * 256, k * 256 + 128), slice(k * 256 + 128, k * 256 + 256)
        for row in range(0, A, TILE):
            rows = slice(row, row + TILE)
            put_pair(k, rows, mul((spec[rows, at], spec[rows, half]), (f_spec[rows, at], f_spec[rows, half])))
        f_spec[:, k * 256 : k * 256 + 256] = inner(bh, bl, k)
    for row in range(0, A, TILE):
        rows, imag = slice(row, row + TILE), slice(A + row, A + row + TILE)
        back = [
            (f_spec[rows, k * 256 : k * 256 + 128], f_spec[rows, k * 256 + 128 : k * 256 + 256]) for k in range(4)
        ]
        for r, value in enumerate(four_point(back, 1.0)):
            at = slice(r * 128, r * 128 + 128)
            re, im = mul_conj(value, (tc[rows, at], ts[rows, at]))
            y_hi[rows, at], y_lo[rows, at] = parts_of(re)
            y_hi[imag, at], y_lo[imag, at] = parts_of(im)

    sides = [wrap(ch + k, N_CH) for k in range(N_CH)]

    def piece_copy(peer, to):
        return pltpu.make_async_remote_copy(
            src_ref=send_y.at[to, peer], dst_ref=recv_y.at[ch, me], send_sem=y_send, recv_sem=y_recv.at[ch],
            device_id=(peer, to), device_id_type=MESH,
        )

    def send_pieces(quarters):
        for offsets in ((4,), (3, 5), (2, 6), (1, 7)):
            bases = [wrap(z + dz, 8) * 8 for dz in offsets]

            def step(i, carry, bases=bases):
                to = wrap(lane + i, 8)
                for y in quarters:
                    for base in bases:
                        piece_copy(base + to, y).start()
                return carry

            lax.fori_loop(0, 8, step, 0, unroll=4 // len(offsets))

        def near(i, carry):
            for y in quarters:
                piece_copy(z * 8 + wrap(lane + i, 8), y).start()
            return carry

        lax.fori_loop(1, 8, near, 0)
        for y in quarters:

            @pl.when(y != ch)
            def _():
                piece_copy(me, y).start()

    for first in (0, 2):
        at = slice(first * 128, first * 128 + 256)
        y = dot(ph[...], y_hi[:, at]) + dot(plo[...], y_hi[:, at]) + dot(ph[...], y_lo[:, at])
        for r in range(2):
            send_y[first + r] = y[:, r * 128 : r * 128 + 128].reshape(N_CTX, PIECES, 128).astype(BF16)
        send_pieces((first, first + 1))
    pltpu.make_async_copy(send_y.at[ch, me], recv_y.at[ch, me], y_recv.at[ch]).start()

    three = pl.ds(0, N_CH - 1)
    to_peer(skip_all.at[three], skip_all.at[three], small_send.at[0], small_recv.at[0], 1).wait_recv()
    to_peer(w_all.at[three], w_all.at[three], small_send.at[1], small_recv.at[1], 1).wait_recv()
    to_peer(side_in.at[three], side_in.at[three], side_send, side_recv, 1).wait_recv()
    eye = lax.broadcasted_iota(jnp.int32, (N_CTX, N_CTX), 0) == lax.broadcasted_iota(jnp.int32, (N_CTX, N_CTX), 1)
    for y in range(N_CH):
        gain = jnp.sum(jnp.where(eye, skip_all[y], 0.0), axis=1, keepdims=True)
        gain_v[y] = gain * side_in[y, 1].astype(F32)

    for y in range(N_CH):
        whole(recv_y.at[y], y_send, y_recv.at[y]).wait_recv()
        conv32[...] = recv_y[y].astype(F32).reshape(N_CTX * PIECES, 128)
        for i in range(PIECES):
            lanes = slice(i * 128, i * 128 + 128)
            c = conv32[pl.ds(i, N_CTX, stride=PIECES), :]
            value = side_in[y, 0, :, lanes].astype(F32) * (c + gain_v[y, :, lanes])
            gated[y * N_CTX : (y + 1) * N_CTX, lanes] = value.astype(BF16)

    mixed = dot(w_all[...].reshape(N_CH * N_CTX, N_CH * N_CTX), gated[...])
    mix_out[...] = mixed.astype(BF16).reshape(N_CH, N_CTX, PIECES * 128)
    for o in (2, 1, 3):
        to_peer(mix_out.at[lax.rem(ch + o, N_CH)], mix_in.at[ch], mix_send, mix_recv, o).start()
    mix_in[ch] = mix_out[ch]
    to_peer(mix_in.at[three], mix_in.at[three], mix_send, mix_recv, 1).wait_recv()
    for y in range(N_CH):
        for i in range(PIECES):
            at = lane_tile(y, i) * 128
            out_ref[:, at : at + 128] = mix_in[y, :, i * 128 : i * 128 + 128]

    to_peer(skip_all.at[three], skip_all.at[three], small_send.at[0], small_recv.at[0], 1).wait_send()
    to_peer(w_all.at[three], w_all.at[three], small_send.at[1], small_recv.at[1], 1).wait_send()
    to_peer(side_in.at[three], side_in.at[three], side_send, side_recv, 1).wait_send()
    to_peer(mix_in.at[three], mix_in.at[three], mix_send, mix_recv, 1).wait_send()
    most = pl.ds(0, N_CTX - 1)
    whole(send_s.at[most], s_send, s_recv).wait_send()
    whole(send_f.at[most], f_send, f_recv).wait_send()
    whole(send_y.at[three], y_send, y_recv.at[0]).wait_send()
    whole(send_y.at[0, most], y_send, y_recv.at[0]).wait_send()


def on_device(value_in, key_gate, query_gate, filter_taps, skip_gain, out_weight):
    consts = tables()
    args = [value_in, key_gate, query_gate, filter_taps, skip_gain.reshape(1, N_CTX), out_weight.T]
    args += [jnp.asarray(c) for c in consts]
    vm = pltpu.VMEM
    copies = [vm((N_CTX, CHUNK), BF16)] * 3 + [vm((N_CTX, CHUNK), F32), vm((1, N_CTX), F32), vm((N_CTX, N_CH * N_CTX), BF16)]
    copies += [vm((N_CH, 1, N_CTX), F32), vm((N_CH, N_CTX, N_CH * N_CTX), BF16)]
    copies += [vm(c.shape, c.dtype) for c in consts]
    copies += [vm((2 * A, A), BF16)] * 2 + [vm((A, 2 * A), BF16)] * 2 + [vm((4, 256, 256), BF16)] * 4 + [vm((A, B), F32)] * 2
    chunk = vm((N_CTX, ROWS, 128), BF16)
    dma = pltpu.SemaphoreType.DMA
    return pl.pallas_call(
        kernel,
        out_shape=jax.ShapeDtypeStruct((N_CTX, CHUNK), BF16),
        in_specs=[pl.BlockSpec(memory_space=pltpu.HBM)] * len(args),
        out_specs=pl.BlockSpec(memory_space=pltpu.VMEM),
        scratch_shapes=copies
        + [vm((N_CTX * ROWS, 128), F32)]
        + [chunk] * 2
        + [vm((N_CH, N_CTX, PIECES, 128), BF16)]
        + [chunk] * 2
        + [vm((N_CH, N_CTX, PIECES, 128), BF16)]
        + [vm((N_CH, 2, N_CTX, CHUNK // N_CH), BF16)] * 2
        + [
            vm((N_CH, N_CTX, CHUNK // N_CH), F32),
            vm((A, B), BF16),
            vm((2 * A, B), F32),
            vm((A, 2 * B), BF16),
            vm((A, 2 * B), BF16),
            vm((A, 2 * B), F32),
            vm((A, 2 * B), F32),
            vm((2 * A, B), BF16),
            vm((2 * A, B), BF16),
            vm((N_CTX * PIECES, 128), F32),
            vm((N_CH * N_CTX, CHUNK // N_CH), BF16),
            vm((N_CH, N_CTX, CHUNK // N_CH), BF16),
            vm((N_CH, N_CTX, CHUNK // N_CH), BF16),
            dma((6,)), dma((10,)), dma, dma, dma, dma, dma, dma((N_CH,)), dma, dma, dma((2,)), dma((2,)),
            dma, dma, pltpu.SemaphoreType.REGULAR,
        ],
        compiler_params=pltpu.CompilerParams(
            collective_id=0, has_side_effects=True, vmem_limit_bytes=56 * 1024 * 1024
        ),
        name="hyena",
    )(*args)


def solution(mesh):
    placed = (
        P("ch", "ctx"),
        P("ch", "ctx"),
        P("ch", "ctx"),
        P("ch", "ctx"),
        P("ch"),
        P(None, "ch"),
    )
    return jax.shard_map(
        on_device, mesh=mesh, in_specs=placed, out_specs=P("ch", "ctx"), check_vma=False
    )
```

```python
import functools

import jax
import jax.numpy as jnp
import numpy as np
from jax import lax
from jax.experimental import pallas as pl
from jax.experimental.pallas import tpu as pltpu
from jax.sharding import PartitionSpec as P

F32 = jnp.float32
BF16 = jnp.bfloat16
MESH = pl.DeviceIdType.MESH

N_CTX = 64
N_CH = 4
CHUNK = 2048
ROWS = 16
T = N_CTX * CHUNK
A = 256
B = 512
PIECES = ROWS // N_CH
TILE = 32


def turns(rows, columns):
    angle = 2 * np.pi * np.outer(rows, columns)
    return np.stack([np.cos(angle), np.sin(angle)]).astype(np.float32)


@functools.cache
def tables():
    coarse, fine = 16 * np.arange(A // 16), np.arange(16)
    freq, column = np.arange(A) + 0.25, np.arange(B)
    inner = (4 * np.arange(128)[None, :] + np.arange(4)[:, None]).reshape(-1) / B
    lanes = np.tile(np.arange(128), 4)
    back = turns(fine, 4 * lanes / B)
    shift = np.repeat(np.arange(4), 128) * lanes / B
    cs, sn = np.cos(2 * np.pi * shift), np.sin(2 * np.pi * shift)
    back = np.stack([back[0] * cs - back[1] * sn, back[1] * cs + back[0] * sn]).astype(np.float32)
    return (
        turns(coarse, np.arange(A) / A), turns(fine + 0.25, np.arange(A) / A),
        turns(coarse, freq / A), turns(fine, freq / A),
        turns(coarse[:8], inner), turns(fine, inner),
        turns(coarse[:8], 4 * lanes / B), back,
        turns(coarse, column / T), turns(fine + 0.25, column / T),
    )


def dot(a, b):
    return jnp.dot(a, b, preferred_element_type=F32)


def parts_of(x):
    high = x.astype(BF16)
    return high, (x - high.astype(F32)).astype(BF16)


def lane_tile(y, i):
    return 4 * i + y


def mul(a, b):
    return a[0] * b[0] - a[1] * b[1], a[0] * b[1] + a[1] * b[0]


def mul_conj(a, b):
    return a[0] * b[0] + a[1] * b[1], a[1] * b[0] - a[0] * b[1]


def add(a, b):
    return a[0] + b[0], a[1] + b[1]


def sub(a, b):
    return a[0] - b[0], a[1] - b[1]


def four_point(x, sign):
    even, odd = add(x[0], x[2]), add(x[1], x[3])
    even_d, odd_d = sub(x[0], x[2]), sub(x[1], x[3])
    turned = (-sign * odd_d[1], sign * odd_d[0])
    return add(even, odd), add(even_d, turned), sub(even, odd), sub(even_d, turned)


def kernel(
    v_hbm, k_hbm, q_hbm, f_hbm, skip_hbm, w_hbm,
    fa_hbm, fb_hbm, ga_hbm, gb_hbm, ia_hbm, ib_hbm, ja_hbm, jb_hbm, ta_hbm, tb_hbm,
    out_ref,
    v_ref, k_ref, q_ref, f_ref, skip_row, w_ref, skip_all, w_all,
    fa, fb, ga, gb, ia, ib, ja, jb, ta, tb,
    oh, ol, ph, plo, ah, al, bh, bl, tc, ts,
    stage, send_s, send_f, send_y, recv_s, recv_f, recv_y,
    side_out, side_in, gain_v, x_ref, z_ref, s_hi, s_lo, spec, f_spec, y_hi, y_lo, conv32, gated, mix_out, mix_in,
    in_sem, table_sem, s_send, s_recv, f_send, f_recv, y_send, y_recv, side_send, side_recv, small_send, small_recv,
    mix_send, mix_recv, ready,
):
    me = lax.axis_index("ctx")
    ch = lax.axis_index("ch")

    barrier = pltpu.get_barrier_semaphore()

    def wrap(value, size):
        return jnp.where(value >= size, value - size, value)

    z, lane = me // 8, me % 8

    def greet(bases):
        def step(i, carry):
            to = wrap(lane + i, 8)
            for base in bases:
                pl.semaphore_signal(barrier, inc=1, device_id=(base + to, ch), device_id_type=MESH)
            return carry

        return step

    away = [[wrap(z + dz, 8) * 8 for dz in offsets] for offsets in ((4,), (3, 5), (2, 6), (1, 7))]
    for bases in away:
        lax.fori_loop(0, 8, greet(bases), 0, unroll=4)
    for o in range(1, N_CH):
        pl.semaphore_signal(barrier, inc=1, device_id=(me, wrap(ch + o, N_CH)), device_id_type=MESH)
    lax.fori_loop(1, 8, greet([z * 8]), 0)

    loads = [
        pltpu.make_async_copy(src, dst, in_sem.at[i])
        for i, (src, dst) in enumerate(
            [(v_hbm, v_ref), (k_hbm, k_ref), (f_hbm, f_ref), (q_hbm, q_ref), (skip_hbm, skip_row), (w_hbm, w_ref)]
        )
    ]
    table_loads = [
        pltpu.make_async_copy(src, dst, table_sem.at[i])
        for i, (src, dst) in enumerate(
            zip(
                (fa_hbm, fb_hbm, ga_hbm, gb_hbm, ia_hbm, ib_hbm, ja_hbm, jb_hbm, ta_hbm, tb_hbm),
                (fa, fb, ga, gb, ia, ib, ja, jb, ta, tb),
            )
        )
    ]
    for copy in loads + table_loads:
        copy.start()

    def to_chunks(value, send):
        for r in range(ROWS):
            stage[pl.ds(r, N_CTX, stride=ROWS), :] = value(r)
        send[...] = stage[...].astype(BF16).reshape(N_CTX, ROWS, 128)

    def tile(ref, r):
        return ref[:, r * 128 : (r + 1) * 128].astype(F32)

    loads[0].wait()
    loads[1].wait()
    to_chunks(lambda r: tile(v_ref, r) * tile(k_ref, r), send_s)
    loads[2].wait()
    to_chunks(lambda r: tile(f_ref, r), send_f)

    pl.semaphore_wait(barrier, N_CTX - 1 + N_CH - 1)
    def chunk_copy(send, recv, s_sem, r_sem, peer):
        return pltpu.make_async_remote_copy(
            src_ref=send.at[peer], dst_ref=recv.at[me], send_sem=s_sem, recv_sem=r_sem,
            device_id=(peer, ch), device_id_type=MESH,
        )

    def scatter(send, recv, s_sem, r_sem):
        for bases in away:

            def step(i, carry, bases=bases):
                to = wrap(lane + i, 8)
                for base in bases:
                    chunk_copy(send, recv, s_sem, r_sem, base + to).start()
                return carry

            lax.fori_loop(0, 8, step, 0, unroll=2)

        def near(i, carry):
            chunk_copy(send, recv, s_sem, r_sem, z * 8 + wrap(lane + i, 8)).start()
            return carry

        lax.fori_loop(1, 8, near, 0)
        pltpu.make_async_copy(send.at[me], recv.at[me], r_sem).start()

    def whole(ref, s_sem, r_sem):
        return pltpu.make_async_remote_copy(
            src_ref=ref, dst_ref=ref, send_sem=s_sem, recv_sem=r_sem,
            device_id=(lax.rem(me + 1, N_CTX), ch), device_id_type=MESH,
        )

    scatter(send_s, recv_s, s_send, s_recv)
    scatter(send_f, recv_f, f_send, f_recv)
    for o in range(1, N_CH):
        pl.semaphore_signal(ready, inc=1, device_id=(me, lax.rem(ch + o, N_CH)), device_id_type=MESH)

    def to_peer(src, dst, s_sem, r_sem, o):
        return pltpu.make_async_remote_copy(
            src_ref=src, dst_ref=dst, send_sem=s_sem, recv_sem=r_sem,
            device_id=(me, lax.rem(ch + o, N_CH)), device_id_type=MESH,
        )

    for copy in loads[3:]:
        copy.wait()
    for y in range(N_CH):
        for i in range(PIECES):
            src = slice(lane_tile(y, i) * 128, lane_tile(y, i) * 128 + 128)
            dst = slice(i * 128, i * 128 + 128)
            side_out[y, 0, :, dst] = q_ref[:, src]
            side_out[y, 1, :, dst] = v_ref[:, src]
    pl.semaphore_wait(ready, N_CH - 1)
    for o in (2, 1, 3):
        to_peer(skip_row, skip_all.at[ch], small_send.at[0], small_recv.at[0], o).start()
        to_peer(w_ref, w_all.at[ch], small_send.at[1], small_recv.at[1], o).start()
        to_peer(side_out.at[lax.rem(ch + o, N_CH)], side_in.at[ch], side_send, side_recv, o).start()
    skip_all[ch] = skip_row[...]
    w_all[ch] = w_ref[...]
    side_in[ch] = side_out[ch]

    for copy in table_loads:
        copy.wait()

    def block(coarse, fine, i):
        ca, sa = coarse[0, pl.ds(i, 1), :], coarse[1, pl.ds(i, 1), :]
        cb, sb = fine[0], fine[1]
        return ca * cb - sa * sb, ca * sb + sa * cb

    def put(high_ref, low_ref, at, value):
        high_ref[at], low_ref[at] = parts_of(value)

    def make_outer(i, carry):
        up = pl.ds(pl.multiple_of(i * 16, 16), 16)
        down = pl.ds(pl.multiple_of(A + i * 16, 16), 16)
        c, s = block(fa, fb, i)
        put(oh, ol, (up,), c)
        put(oh, ol, (down,), -s)
        c, s = block(ga, gb, i)
        put(ph, plo, (up, slice(0, A)), c * (1.0 / T))
        put(ph, plo, (up, slice(A, 2 * A)), s * (-1.0 / T))
        c, s = block(ta, tb, i)
        tc[up, :], ts[up, :] = c, -s
        return carry

    def make_inner(i, carry):
        up = pl.ds(pl.multiple_of(i * 16, 16), 16)
        down = pl.ds(pl.multiple_of(128 + i * 16, 16), 16)
        left, right = slice(0, 128), slice(128, 256)
        for high, low, coarse, fine, sign in ((ah, al, ia, ib, 1.0), (bh, bl, ja, jb, -1.0)):
            c, s = block(coarse, fine, i)
            for k in range(4):
                ck, sk = c[:, k * 128 : k * 128 + 128], s[:, k * 128 : k * 128 + 128]
                put(high, low, (k, up, left), ck)
                put(high, low, (k, down, right), ck)
                put(high, low, (k, up, right), -sign * sk)
                put(high, low, (k, down, left), sign * sk)
        return carry

    lax.fori_loop(0, A // 16, make_outer, 0)
    lax.fori_loop(0, 8, make_inner, 0)

    def load_matrix(recv):
        stage[...] = recv[...].astype(F32).reshape(N_CTX * ROWS, 128)
        for r in range(4):
            x_ref[:, r * 128 : r * 128 + 128] = stage[pl.ds(r, A, stride=4), :].astype(BF16)

    def pair(ref, rows, k, imag):
        return ref[rows, k * 128 : k * 128 + 128], ref[imag, k * 128 : k * 128 + 128]

    def put_pair(k, rows, value):
        for part, at in ((value[0], k * 256), (value[1], k * 256 + 128)):
            s_hi[rows, at : at + 128], s_lo[rows, at : at + 128] = parts_of(part)

    def inner(high, low, k):
        at = slice(k * 256, k * 256 + 256)
        return dot(s_hi[:, at], high[k]) + dot(s_hi[:, at], low[k]) + dot(s_lo[:, at], high[k])

    def forward(recv, out):
        load_matrix(recv)
        z_ref[...] = dot(oh[...], x_ref[...]) + dot(ol[...], x_ref[...])
        for row in range(0, A, TILE):
            rows, imag = slice(row, row + TILE), slice(A + row, A + row + TILE)
            turned = []
            for r in range(4):
                at = slice(r * 128, r * 128 + 128)
                turned.append(mul(pair(z_ref, rows, r, imag), (tc[rows, at], ts[rows, at])))
            for k, value in enumerate(four_point(turned, -1.0)):
                put_pair(k, rows, value)
        for k in range(4):
            out[:, k * 256 : k * 256 + 256] = inner(ah, al, k)

    whole(recv_s, s_send, s_recv).wait_recv()
    forward(recv_s, spec)

    whole(recv_f, f_send, f_recv).wait_recv()
    forward(recv_f, f_spec)
    for k in range(4):
        at, half = slice(k * 256, k * 256 + 128), slice(k * 256 + 128, k * 256 + 256)
        for row in range(0, A, TILE):
            rows = slice(row, row + TILE)
            put_pair(k, rows, mul((spec[rows, at], spec[rows, half]), (f_spec[rows, at], f_spec[rows, half])))
        f_spec[:, k * 256 : k * 256 + 256] = inner(bh, bl, k)
    for row in range(0, A, TILE):
        rows, imag = slice(row, row + TILE), slice(A + row, A + row + TILE)
        back = [
            (f_spec[rows, k * 256 : k * 256 + 128], f_spec[rows, k * 256 + 128 : k * 256 + 256]) for k in range(4)
        ]
        for r, value in enumerate(four_point(back, 1.0)):
            at = slice(r * 128, r * 128 + 128)
            re, im = mul_conj(value, (tc[rows, at], ts[rows, at]))
            y_hi[rows, at], y_lo[rows, at] = parts_of(re)
            y_hi[imag, at], y_lo[imag, at] = parts_of(im)

    sides = [wrap(ch + k, N_CH) for k in range(N_CH)]

    def piece_copy(peer, to):
        return pltpu.make_async_remote_copy(
            src_ref=send_y.at[to, peer], dst_ref=recv_y.at[ch, me], send_sem=y_send, recv_sem=y_recv.at[ch],
            device_id=(peer, to), device_id_type=MESH,
        )

    for first in (0, 2):
        at = slice(first * 128, first * 128 + 256)
        y = dot(ph[...], y_hi[:, at]) + dot(plo[...], y_hi[:, at]) + dot(ph[...], y_lo[:, at])
        for r in range(2):
            send_y[first + r] = y[:, r * 128 : r * 128 + 128].reshape(N_CTX, PIECES, 128).astype(BF16)

    for to_z in (0, 1, 2, 3, 4, 7, 5, 6):

        def step(i, carry, base=to_z * 8):
            peer = base + wrap(lane + i, 8)
            for k in (2, 1, 3):
                piece_copy(peer, sides[k]).start()

            @pl.when(peer != me)
            def _():
                piece_copy(peer, ch).start()

            return carry

        lax.fori_loop(0, 8, step, 0, unroll=2)
    pltpu.make_async_copy(send_y.at[ch, me], recv_y.at[ch, me], y_recv.at[ch]).start()

    three = pl.ds(0, N_CH - 1)
    to_peer(skip_all.at[three], skip_all.at[three], small_send.at[0], small_recv.at[0], 1).wait_recv()
    to_peer(w_all.at[three], w_all.at[three], small_send.at[1], small_recv.at[1], 1).wait_recv()
    to_peer(side_in.at[three], side_in.at[three], side_send, side_recv, 1).wait_recv()
    eye = lax.broadcasted_iota(jnp.int32, (N_CTX, N_CTX), 0) == lax.broadcasted_iota(jnp.int32, (N_CTX, N_CTX), 1)
    for y in range(N_CH):
        gain = jnp.sum(jnp.where(eye, skip_all[y], 0.0), axis=1, keepdims=True)
        gain_v[y] = gain * side_in[y, 1].astype(F32)

    for y in range(N_CH):
        whole(recv_y.at[y], y_send, y_recv.at[y]).wait_recv()
        conv32[...] = recv_y[y].astype(F32).reshape(N_CTX * PIECES, 128)
        for i in range(PIECES):
            lanes = slice(i * 128, i * 128 + 128)
            c = conv32[pl.ds(i, N_CTX, stride=PIECES), :]
            value = side_in[y, 0, :, lanes].astype(F32) * (c + gain_v[y, :, lanes])
            gated[y * N_CTX : (y + 1) * N_CTX, lanes] = value.astype(BF16)

    mixed = dot(w_all[...].reshape(N_CH * N_CTX, N_CH * N_CTX), gated[...])
    mix_out[...] = mixed.astype(BF16).reshape(N_CH, N_CTX, PIECES * 128)
    for o in (2, 1, 3):
        to_peer(mix_out.at[lax.rem(ch + o, N_CH)], mix_in.at[ch], mix_send, mix_recv, o).start()
    mix_in[ch] = mix_out[ch]
    to_peer(mix_in.at[three], mix_in.at[three], mix_send, mix_recv, 1).wait_recv()
    for y in range(N_CH):
        for i in range(PIECES):
            at = lane_tile(y, i) * 128
            out_ref[:, at : at + 128] = mix_in[y, :, i * 128 : i * 128 + 128]

    to_peer(skip_all.at[three], skip_all.at[three], small_send.at[0], small_recv.at[0], 1).wait_send()
    to_peer(w_all.at[three], w_all.at[three], small_send.at[1], small_recv.at[1], 1).wait_send()
    to_peer(side_in.at[three], side_in.at[three], side_send, side_recv, 1).wait_send()
    to_peer(mix_in.at[three], mix_in.at[three], mix_send, mix_recv, 1).wait_send()
    most = pl.ds(0, N_CTX - 1)
    whole(send_s.at[most], s_send, s_recv).wait_send()
    whole(send_f.at[most], f_send, f_recv).wait_send()
    whole(send_y.at[three], y_send, y_recv.at[0]).wait_send()
    whole(send_y.at[0, most], y_send, y_recv.at[0]).wait_send()


def on_device(value_in, key_gate, query_gate, filter_taps, skip_gain, out_weight):
    consts = tables()
    args = [value_in, key_gate, query_gate, filter_taps, skip_gain.reshape(1, N_CTX), out_weight.T]
    args += [jnp.asarray(c) for c in consts]
    vm = pltpu.VMEM
    copies = [vm((N_CTX, CHUNK), BF16)] * 3 + [vm((N_CTX, CHUNK), F32), vm((1, N_CTX), F32), vm((N_CTX, N_CH * N_CTX), BF16)]
    copies += [vm((N_CH, 1, N_CTX), F32), vm((N_CH, N_CTX, N_CH * N_CTX), BF16)]
    copies += [vm(c.shape, c.dtype) for c in consts]
    copies += [vm((2 * A, A), BF16)] * 2 + [vm((A, 2 * A), BF16)] * 2 + [vm((4, 256, 256), BF16)] * 4 + [vm((A, B), F32)] * 2
    chunk = vm((N_CTX, ROWS, 128), BF16)
    dma = pltpu.SemaphoreType.DMA
    return pl.pallas_call(
        kernel,
        out_shape=jax.ShapeDtypeStruct((N_CTX, CHUNK), BF16),
        in_specs=[pl.BlockSpec(memory_space=pltpu.HBM)] * len(args),
        out_specs=pl.BlockSpec(memory_space=pltpu.VMEM),
        scratch_shapes=copies
        + [vm((N_CTX * ROWS, 128), F32)]
        + [chunk] * 2
        + [vm((N_CH, N_CTX, PIECES, 128), BF16)]
        + [chunk] * 2
        + [vm((N_CH, N_CTX, PIECES, 128), BF16)]
        + [vm((N_CH, 2, N_CTX, CHUNK // N_CH), BF16)] * 2
        + [
            vm((N_CH, N_CTX, CHUNK // N_CH), F32),
            vm((A, B), BF16),
            vm((2 * A, B), F32),
            vm((A, 2 * B), BF16),
            vm((A, 2 * B), BF16),
            vm((A, 2 * B), F32),
            vm((A, 2 * B), F32),
            vm((2 * A, B), BF16),
            vm((2 * A, B), BF16),
            vm((N_CTX * PIECES, 128), F32),
            vm((N_CH * N_CTX, CHUNK // N_CH), BF16),
            vm((N_CH, N_CTX, CHUNK // N_CH), BF16),
            vm((N_CH, N_CTX, CHUNK // N_CH), BF16),
            dma((6,)), dma((10,)), dma, dma, dma, dma, dma, dma((N_CH,)), dma, dma, dma((2,)), dma((2,)),
            dma, dma, pltpu.SemaphoreType.REGULAR,
        ],
        compiler_params=pltpu.CompilerParams(
            collective_id=0, has_side_effects=True, vmem_limit_bytes=56 * 1024 * 1024
        ),
        name="hyena",
    )(*args)


def solution(mesh):
    placed = (
        P("ch", "ctx"),
        P("ch", "ctx"),
        P("ch", "ctx"),
        P("ch", "ctx"),
        P("ch"),
        P(None, "ch"),
    )
    return jax.shard_map(
        on_device, mesh=mesh, in_specs=placed, out_specs=P("ch", "ctx"), check_vma=False
    )
```

```python
import functools

import jax
import jax.numpy as jnp
import numpy as np
from jax import lax
from jax.experimental import pallas as pl
from jax.experimental.pallas import tpu as pltpu
from jax.sharding import PartitionSpec as P

F32 = jnp.float32
BF16 = jnp.bfloat16
MESH = pl.DeviceIdType.MESH

N_CTX = 64
N_CH = 4
CHUNK = 2048
ROWS = 16
T = N_CTX * CHUNK
A = 256
B = 512
PIECES = ROWS // N_CH
TILE = 32


def turns(rows, columns):
    angle = 2 * np.pi * np.outer(rows, columns)
    return np.stack([np.cos(angle), np.sin(angle)]).astype(np.float32)


@functools.cache
def tables():
    coarse, fine = 16 * np.arange(A // 16), np.arange(16)
    freq, column = np.arange(A) + 0.25, np.arange(B)
    inner = (4 * np.arange(128)[None, :] + np.arange(4)[:, None]).reshape(-1) / B
    lanes = np.tile(np.arange(128), 4)
    back = turns(fine, 4 * lanes / B)
    shift = np.repeat(np.arange(4), 128) * lanes / B
    cs, sn = np.cos(2 * np.pi * shift), np.sin(2 * np.pi * shift)
    back = np.stack([back[0] * cs - back[1] * sn, back[1] * cs + back[0] * sn]).astype(np.float32)
    return (
        turns(coarse, np.arange(A) / A), turns(fine + 0.25, np.arange(A) / A),
        turns(coarse, freq / A), turns(fine, freq / A),
        turns(coarse[:8], inner), turns(fine, inner),
        turns(coarse[:8], 4 * lanes / B), back,
        turns(coarse, column / T), turns(fine + 0.25, column / T),
    )


def dot(a, b):
    return jnp.dot(a, b, preferred_element_type=F32)


def parts_of(x):
    high = x.astype(BF16)
    return high, (x - high.astype(F32)).astype(BF16)


def lane_tile(y, i):
    return 4 * i + y


def mul(a, b):
    return a[0] * b[0] - a[1] * b[1], a[0] * b[1] + a[1] * b[0]


def mul_conj(a, b):
    return a[0] * b[0] + a[1] * b[1], a[1] * b[0] - a[0] * b[1]


def add(a, b):
    return a[0] + b[0], a[1] + b[1]


def sub(a, b):
    return a[0] - b[0], a[1] - b[1]


def four_point(x, sign):
    even, odd = add(x[0], x[2]), add(x[1], x[3])
    even_d, odd_d = sub(x[0], x[2]), sub(x[1], x[3])
    turned = (-sign * odd_d[1], sign * odd_d[0])
    return add(even, odd), add(even_d, turned), sub(even, odd), sub(even_d, turned)


def kernel(
    v_hbm, k_hbm, q_hbm, f_hbm, skip_hbm, w_hbm,
    fa_hbm, fb_hbm, ga_hbm, gb_hbm, ia_hbm, ib_hbm, ja_hbm, jb_hbm, ta_hbm, tb_hbm,
    out_ref,
    v_ref, k_ref, q_ref, f_ref, skip_row, w_ref, skip_all, w_all,
    fa, fb, ga, gb, ia, ib, ja, jb, ta, tb,
    oh, ol, ph, plo, ah, al, bh, bl, tc, ts,
    stage, send_s, send_f, send_y, recv_s, recv_f, recv_y,
    side_out, side_in, gain_v, x_ref, z_ref, s_hi, s_lo, spec, f_spec, y_hi, y_lo, conv32, gated, mix_out, mix_in,
    in_sem, table_sem, s_send, s_recv, f_send, f_recv, y_send, y_recv, side_send, side_recv, small_send, small_recv,
    mix_send, mix_recv, ready,
):
    me = lax.axis_index("ctx")
    ch = lax.axis_index("ch")

    barrier = pltpu.get_barrier_semaphore()

    def wrap(value, size):
        return jnp.where(value >= size, value - size, value)

    z, lane = me // 8, me % 8

    def greet(bases):
        def step(i, carry):
            to = wrap(lane + i, 8)
            for base in bases:
                pl.semaphore_signal(barrier, inc=1, device_id=(base + to, ch), device_id_type=MESH)
            return carry

        return step

    away = [[wrap(z + dz, 8) * 8 for dz in offsets] for offsets in ((4,), (3, 5), (2, 6), (1, 7))]
    for bases in away:
        lax.fori_loop(0, 8, greet(bases), 0, unroll=4)
    for o in range(1, N_CH):
        pl.semaphore_signal(barrier, inc=1, device_id=(me, wrap(ch + o, N_CH)), device_id_type=MESH)
    lax.fori_loop(1, 8, greet([z * 8]), 0)

    loads = [
        pltpu.make_async_copy(src, dst, in_sem.at[i])
        for i, (src, dst) in enumerate(
            [(v_hbm, v_ref), (k_hbm, k_ref), (f_hbm, f_ref), (q_hbm, q_ref), (skip_hbm, skip_row), (w_hbm, w_ref)]
        )
    ]
    table_loads = [
        pltpu.make_async_copy(src, dst, table_sem.at[i])
        for i, (src, dst) in enumerate(
            zip(
                (fa_hbm, fb_hbm, ga_hbm, gb_hbm, ia_hbm, ib_hbm, ja_hbm, jb_hbm, ta_hbm, tb_hbm),
                (fa, fb, ga, gb, ia, ib, ja, jb, ta, tb),
            )
        )
    ]
    for copy in loads + table_loads:
        copy.start()

    def to_chunks(value, send):
        for r in range(ROWS):
            stage[pl.ds(r, N_CTX, stride=ROWS), :] = value(r)
        send[...] = stage[...].astype(BF16).reshape(N_CTX, ROWS, 128)

    def tile(ref, r):
        return ref[:, r * 128 : (r + 1) * 128].astype(F32)

    loads[0].wait()
    loads[1].wait()
    to_chunks(lambda r: tile(v_ref, r) * tile(k_ref, r), send_s)
    loads[2].wait()
    to_chunks(lambda r: tile(f_ref, r), send_f)

    pl.semaphore_wait(barrier, N_CTX - 1 + N_CH - 1)
    def chunk_copy(send, recv, s_sem, r_sem, peer):
        return pltpu.make_async_remote_copy(
            src_ref=send.at[peer], dst_ref=recv.at[me], send_sem=s_sem, recv_sem=r_sem,
            device_id=(peer, ch), device_id_type=MESH,
        )

    def scatter(send, recv, s_sem, r_sem, core):
        for bases in away:

            def step(i, carry, bases=bases):
                to = wrap(lane // 2 + i, 4) * 2 + core
                for base in bases:
                    chunk_copy(send, recv, s_sem, r_sem, base + to).start()
                return carry

            lax.fori_loop(0, 4, step, 0, unroll=2)

        def near(i, carry):
            peer = z * 8 + wrap(lane // 2 + i, 4) * 2 + core

            @pl.when(peer != me)
            def _():
                chunk_copy(send, recv, s_sem, r_sem, peer).start()

            return carry

        lax.fori_loop(0, 4, near, 0)

    def whole(ref, s_sem, r_sem):
        return pltpu.make_async_remote_copy(
            src_ref=ref, dst_ref=ref, send_sem=s_sem, recv_sem=r_sem,
            device_id=(lax.rem(me + 1, N_CTX), ch), device_id_type=MESH,
        )

    def scatter_both(core, carry):
        scatter(send_s, recv_s, s_send, s_recv, core)
        scatter(send_f, recv_f, f_send, f_recv, core)
        return carry

    lax.fori_loop(0, 2, scatter_both, 0)
    pltpu.make_async_copy(send_s.at[me], recv_s.at[me], s_recv).start()
    pltpu.make_async_copy(send_f.at[me], recv_f.at[me], f_recv).start()
    for o in range(1, N_CH):
        pl.semaphore_signal(ready, inc=1, device_id=(me, lax.rem(ch + o, N_CH)), device_id_type=MESH)

    def to_peer(src, dst, s_sem, r_sem, o):
        return pltpu.make_async_remote_copy(
            src_ref=src, dst_ref=dst, send_sem=s_sem, recv_sem=r_sem,
            device_id=(me, lax.rem(ch + o, N_CH)), device_id_type=MESH,
        )

    for copy in loads[3:]:
        copy.wait()
    for y in range(N_CH):
        for i in range(PIECES):
            src = slice(lane_tile(y, i) * 128, lane_tile(y, i) * 128 + 128)
            dst = slice(i * 128, i * 128 + 128)
            side_out[y, 0, :, dst] = q_ref[:, src]
            side_out[y, 1, :, dst] = v_ref[:, src]
    pl.semaphore_wait(ready, N_CH - 1)
    for o in (2, 1, 3):
        to_peer(skip_row, skip_all.at[ch], small_send.at[0], small_recv.at[0], o).start()
        to_peer(w_ref, w_all.at[ch], small_send.at[1], small_recv.at[1], o).start()
        to_peer(side_out.at[lax.rem(ch + o, N_CH)], side_in.at[ch], side_send, side_recv, o).start()
    skip_all[ch] = skip_row[...]
    w_all[ch] = w_ref[...]
    side_in[ch] = side_out[ch]

    for copy in table_loads:
        copy.wait()

    def block(coarse, fine, i):
        ca, sa = coarse[0, pl.ds(i, 1), :], coarse[1, pl.ds(i, 1), :]
        cb, sb = fine[0], fine[1]
        return ca * cb - sa * sb, ca * sb + sa * cb

    def put(high_ref, low_ref, at, value):
        high_ref[at], low_ref[at] = parts_of(value)

    def make_outer(i, carry):
        up = pl.ds(pl.multiple_of(i * 16, 16), 16)
        down = pl.ds(pl.multiple_of(A + i * 16, 16), 16)
        c, s = block(fa, fb, i)
        put(oh, ol, (up,), c)
        put(oh, ol, (down,), -s)
        c, s = block(ga, gb, i)
        put(ph, plo, (up, slice(0, A)), c * (1.0 / T))
        put(ph, plo, (up, slice(A, 2 * A)), s * (-1.0 / T))
        c, s = block(ta, tb, i)
        tc[up, :], ts[up, :] = c, -s
        return carry

    def make_inner(i, carry):
        up = pl.ds(pl.multiple_of(i * 16, 16), 16)
        down = pl.ds(pl.multiple_of(128 + i * 16, 16), 16)
        left, right = slice(0, 128), slice(128, 256)
        for high, low, coarse, fine, sign in ((ah, al, ia, ib, 1.0), (bh, bl, ja, jb, -1.0)):
            c, s = block(coarse, fine, i)
            for k in range(4):
                ck, sk = c[:, k * 128 : k * 128 + 128], s[:, k * 128 : k * 128 + 128]
                put(high, low, (k, up, left), ck)
                put(high, low, (k, down, right), ck)
                put(high, low, (k, up, right), -sign * sk)
                put(high, low, (k, down, left), sign * sk)
        return carry

    lax.fori_loop(0, A // 16, make_outer, 0)
    lax.fori_loop(0, 8, make_inner, 0)

    def load_matrix(recv):
        stage[...] = recv[...].astype(F32).reshape(N_CTX * ROWS, 128)
        for r in range(4):
            x_ref[:, r * 128 : r * 128 + 128] = stage[pl.ds(r, A, stride=4), :].astype(BF16)

    def pair(ref, rows, k, imag):
        return ref[rows, k * 128 : k * 128 + 128], ref[imag, k * 128 : k * 128 + 128]

    def put_pair(k, rows, value):
        for part, at in ((value[0], k * 256), (value[1], k * 256 + 128)):
            s_hi[rows, at : at + 128], s_lo[rows, at : at + 128] = parts_of(part)

    def inner(high, low, k):
        at = slice(k * 256, k * 256 + 256)
        return dot(s_hi[:, at], high[k]) + dot(s_hi[:, at], low[k]) + dot(s_lo[:, at], high[k])

    def forward(recv, out):
        load_matrix(recv)
        z_ref[...] = dot(oh[...], x_ref[...]) + dot(ol[...], x_ref[...])
        for row in range(0, A, TILE):
            rows, imag = slice(row, row + TILE), slice(A + row, A + row + TILE)
            turned = []
            for r in range(4):
                at = slice(r * 128, r * 128 + 128)
                turned.append(mul(pair(z_ref, rows, r, imag), (tc[rows, at], ts[rows, at])))
            for k, value in enumerate(four_point(turned, -1.0)):
                put_pair(k, rows, value)
        for k in range(4):
            out[:, k * 256 : k * 256 + 256] = inner(ah, al, k)

    whole(recv_s, s_send, s_recv).wait_recv()
    forward(recv_s, spec)

    whole(recv_f, f_send, f_recv).wait_recv()
    forward(recv_f, f_spec)
    for k in range(4):
        at, half = slice(k * 256, k * 256 + 128), slice(k * 256 + 128, k * 256 + 256)
        for row in range(0, A, TILE):
            rows = slice(row, row + TILE)
            put_pair(k, rows, mul((spec[rows, at], spec[rows, half]), (f_spec[rows, at], f_spec[rows, half])))
        f_spec[:, k * 256 : k * 256 + 256] = inner(bh, bl, k)
    for row in range(0, A, TILE):
        rows, imag = slice(row, row + TILE), slice(A + row, A + row + TILE)
        back = [
            (f_spec[rows, k * 256 : k * 256 + 128], f_spec[rows, k * 256 + 128 : k * 256 + 256]) for k in range(4)
        ]
        for r, value in enumerate(four_point(back, 1.0)):
            at = slice(r * 128, r * 128 + 128)
            re, im = mul_conj(value, (tc[rows, at], ts[rows, at]))
            y_hi[rows, at], y_lo[rows, at] = parts_of(re)
            y_hi[imag, at], y_lo[imag, at] = parts_of(im)

    sides = [wrap(ch + k, N_CH) for k in range(N_CH)]

    def piece_copy(peer, to):
        return pltpu.make_async_remote_copy(
            src_ref=send_y.at[to, peer], dst_ref=recv_y.at[ch, me], send_sem=y_send, recv_sem=y_recv.at[ch],
            device_id=(peer, to), device_id_type=MESH,
        )

    for first in (0, 2):
        at = slice(first * 128, first * 128 + 256)
        y = dot(ph[...], y_hi[:, at]) + dot(plo[...], y_hi[:, at]) + dot(ph[...], y_lo[:, at])
        for r in range(2):
            send_y[first + r] = y[:, r * 128 : r * 128 + 128].reshape(N_CTX, PIECES, 128).astype(BF16)

    for to_z in (0, 1, 2, 3, 4, 7, 5, 6):

        def step(i, carry, base=to_z * 8):
            peer = base + wrap(lane + i, 8)
            for k in (2, 1, 3):
                piece_copy(peer, sides[k]).start()

            @pl.when(peer != me)
            def _():
                piece_copy(peer, ch).start()

            return carry

        lax.fori_loop(0, 8, step, 0, unroll=2)
    pltpu.make_async_copy(send_y.at[ch, me], recv_y.at[ch, me], y_recv.at[ch]).start()

    three = pl.ds(0, N_CH - 1)
    to_peer(skip_all.at[three], skip_all.at[three], small_send.at[0], small_recv.at[0], 1).wait_recv()
    to_peer(w_all.at[three], w_all.at[three], small_send.at[1], small_recv.at[1], 1).wait_recv()
    to_peer(side_in.at[three], side_in.at[three], side_send, side_recv, 1).wait_recv()
    eye = lax.broadcasted_iota(jnp.int32, (N_CTX, N_CTX), 0) == lax.broadcasted_iota(jnp.int32, (N_CTX, N_CTX), 1)
    for y in range(N_CH):
        gain = jnp.sum(jnp.where(eye, skip_all[y], 0.0), axis=1, keepdims=True)
        gain_v[y] = gain * side_in[y, 1].astype(F32)

    for y in range(N_CH):
        whole(recv_y.at[y], y_send, y_recv.at[y]).wait_recv()
        conv32[...] = recv_y[y].astype(F32).reshape(N_CTX * PIECES, 128)
        for i in range(PIECES):
            lanes = slice(i * 128, i * 128 + 128)
            c = conv32[pl.ds(i, N_CTX, stride=PIECES), :]
            value = side_in[y, 0, :, lanes].astype(F32) * (c + gain_v[y, :, lanes])
            gated[y * N_CTX : (y + 1) * N_CTX, lanes] = value.astype(BF16)

    mixed = dot(w_all[...].reshape(N_CH * N_CTX, N_CH * N_CTX), gated[...])
    mix_out[...] = mixed.astype(BF16).reshape(N_CH, N_CTX, PIECES * 128)
    for o in (2, 1, 3):
        to_peer(mix_out.at[lax.rem(ch + o, N_CH)], mix_in.at[ch], mix_send, mix_recv, o).start()
    mix_in[ch] = mix_out[ch]
    to_peer(mix_in.at[three], mix_in.at[three], mix_send, mix_recv, 1).wait_recv()
    for y in range(N_CH):
        for i in range(PIECES):
            at = lane_tile(y, i) * 128
            out_ref[:, at : at + 128] = mix_in[y, :, i * 128 : i * 128 + 128]

    to_peer(skip_all.at[three], skip_all.at[three], small_send.at[0], small_recv.at[0], 1).wait_send()
    to_peer(w_all.at[three], w_all.at[three], small_send.at[1], small_recv.at[1], 1).wait_send()
    to_peer(side_in.at[three], side_in.at[three], side_send, side_recv, 1).wait_send()
    to_peer(mix_in.at[three], mix_in.at[three], mix_send, mix_recv, 1).wait_send()
    most = pl.ds(0, N_CTX - 1)
    whole(send_s.at[most], s_send, s_recv).wait_send()
    whole(send_f.at[most], f_send, f_recv).wait_send()
    whole(send_y.at[three], y_send, y_recv.at[0]).wait_send()
    whole(send_y.at[0, most], y_send, y_recv.at[0]).wait_send()


def on_device(value_in, key_gate, query_gate, filter_taps, skip_gain, out_weight):
    consts = tables()
    args = [value_in, key_gate, query_gate, filter_taps, skip_gain.reshape(1, N_CTX), out_weight.T]
    args += [jnp.asarray(c) for c in consts]
    vm = pltpu.VMEM
    copies = [vm((N_CTX, CHUNK), BF16)] * 3 + [vm((N_CTX, CHUNK), F32), vm((1, N_CTX), F32), vm((N_CTX, N_CH * N_CTX), BF16)]
    copies += [vm((N_CH, 1, N_CTX), F32), vm((N_CH, N_CTX, N_CH * N_CTX), BF16)]
    copies += [vm(c.shape, c.dtype) for c in consts]
    copies += [vm((2 * A, A), BF16)] * 2 + [vm((A, 2 * A), BF16)] * 2 + [vm((4, 256, 256), BF16)] * 4 + [vm((A, B), F32)] * 2
    chunk = vm((N_CTX, ROWS, 128), BF16)
    dma = pltpu.SemaphoreType.DMA
    return pl.pallas_call(
        kernel,
        out_shape=jax.ShapeDtypeStruct((N_CTX, CHUNK), BF16),
        in_specs=[pl.BlockSpec(memory_space=pltpu.HBM)] * len(args),
        out_specs=pl.BlockSpec(memory_space=pltpu.VMEM),
        scratch_shapes=copies
        + [vm((N_CTX * ROWS, 128), F32)]
        + [chunk] * 2
        + [vm((N_CH, N_CTX, PIECES, 128), BF16)]
        + [chunk] * 2
        + [vm((N_CH, N_CTX, PIECES, 128), BF16)]
        + [vm((N_CH, 2, N_CTX, CHUNK // N_CH), BF16)] * 2
        + [
            vm((N_CH, N_CTX, CHUNK // N_CH), F32),
            vm((A, B), BF16),
            vm((2 * A, B), F32),
            vm((A, 2 * B), BF16),
            vm((A, 2 * B), BF16),
            vm((A, 2 * B), F32),
            vm((A, 2 * B), F32),
            vm((2 * A, B), BF16),
            vm((2 * A, B), BF16),
            vm((N_CTX * PIECES, 128), F32),
            vm((N_CH * N_CTX, CHUNK // N_CH), BF16),
            vm((N_CH, N_CTX, CHUNK // N_CH), BF16),
            vm((N_CH, N_CTX, CHUNK // N_CH), BF16),
            dma((6,)), dma((10,)), dma, dma, dma, dma, dma, dma((N_CH,)), dma, dma, dma((2,)), dma((2,)),
            dma, dma, pltpu.SemaphoreType.REGULAR,
        ],
        compiler_params=pltpu.CompilerParams(
            collective_id=0, has_side_effects=True, vmem_limit_bytes=56 * 1024 * 1024
        ),
        name="hyena",
    )(*args)


def solution(mesh):
    placed = (
        P("ch", "ctx"),
        P("ch", "ctx"),
        P("ch", "ctx"),
        P("ch", "ctx"),
        P("ch"),
        P(None, "ch"),
    )
    return jax.shard_map(
        on_device, mesh=mesh, in_specs=placed, out_specs=P("ch", "ctx"), check_vma=False
    )
```

```python
import functools

import jax
import jax.numpy as jnp
import numpy as np
from jax import lax
from jax.experimental import pallas as pl
from jax.experimental.pallas import tpu as pltpu
from jax.sharding import PartitionSpec as P

F32 = jnp.float32
BF16 = jnp.bfloat16
MESH = pl.DeviceIdType.MESH

N_CTX = 64
N_CH = 4
CHUNK = 2048
ROWS = 16
T = N_CTX * CHUNK
A = 256
B = 512
PIECES = ROWS // N_CH
TILE = 32


def turns(rows, columns):
    angle = 2 * np.pi * np.outer(rows, columns)
    return np.stack([np.cos(angle), np.sin(angle)]).astype(np.float32)


@functools.cache
def tables():
    coarse, fine = 16 * np.arange(A // 16), np.arange(16)
    freq, column = np.arange(A) + 0.25, np.arange(B)
    inner = (4 * np.arange(128)[None, :] + np.arange(4)[:, None]).reshape(-1) / B
    lanes = np.tile(np.arange(128), 4)
    back = turns(fine, 4 * lanes / B)
    shift = np.repeat(np.arange(4), 128) * lanes / B
    cs, sn = np.cos(2 * np.pi * shift), np.sin(2 * np.pi * shift)
    back = np.stack([back[0] * cs - back[1] * sn, back[1] * cs + back[0] * sn]).astype(np.float32)
    return (
        turns(coarse, np.arange(A) / A), turns(fine + 0.25, np.arange(A) / A),
        turns(coarse, freq / A), turns(fine, freq / A),
        turns(coarse[:8], inner), turns(fine, inner),
        turns(coarse[:8], 4 * lanes / B), back,
        turns(coarse, column / T), turns(fine + 0.25, column / T),
    )


def dot(a, b):
    return jnp.dot(a, b, preferred_element_type=F32)


def parts_of(x):
    high = x.astype(BF16)
    return high, (x - high.astype(F32)).astype(BF16)


def lane_tile(y, i):
    return 4 * i + y


def mul(a, b):
    return a[0] * b[0] - a[1] * b[1], a[0] * b[1] + a[1] * b[0]


def mul_conj(a, b):
    return a[0] * b[0] + a[1] * b[1], a[1] * b[0] - a[0] * b[1]


def add(a, b):
    return a[0] + b[0], a[1] + b[1]


def sub(a, b):
    return a[0] - b[0], a[1] - b[1]


def four_point(x, sign):
    even, odd = add(x[0], x[2]), add(x[1], x[3])
    even_d, odd_d = sub(x[0], x[2]), sub(x[1], x[3])
    turned = (-sign * odd_d[1], sign * odd_d[0])
    return add(even, odd), add(even_d, turned), sub(even, odd), sub(even_d, turned)


def kernel(
    v_hbm, k_hbm, q_hbm, f_hbm, skip_hbm, w_hbm,
    fa_hbm, fb_hbm, ga_hbm, gb_hbm, ia_hbm, ib_hbm, ja_hbm, jb_hbm, ta_hbm, tb_hbm,
    out_ref,
    v_ref, k_ref, q_ref, f_ref, skip_row, w_ref, skip_all, w_all,
    fa, fb, ga, gb, ia, ib, ja, jb, ta, tb,
    oh, ol, ph, plo, ah, al, bh, bl, tc, ts,
    stage, send_s, send_f, send_y, recv_s, recv_f, recv_y,
    side_out, side_in, gain_v, x_ref, z_ref, s_hi, s_lo, spec, f_spec, y_hi, y_lo, conv32, gated, mix_out, mix_in,
    in_sem, table_sem, s_send, s_recv, f_send, f_recv, y_send, y_recv, side_send, side_recv, small_send, small_recv,
    mix_send, mix_recv, ready,
):
    me = lax.axis_index("ctx")
    ch = lax.axis_index("ch")

    barrier = pltpu.get_barrier_semaphore()

    def wrap(value, size):
        return jnp.where(value >= size, value - size, value)

    z, lane = me // 8, me % 8

    def greet(bases):
        def step(i, carry):
            to = wrap(lane + i, 8)
            for base in bases:
                pl.semaphore_signal(barrier, inc=1, device_id=(base + to, ch), device_id_type=MESH)
            return carry

        return step

    away = [[wrap(z + dz, 8) * 8 for dz in offsets] for offsets in ((4,), (3, 5), (2, 6), (1, 7))]
    for bases in away:
        lax.fori_loop(0, 8, greet(bases), 0, unroll=4)
    for o in range(1, N_CH):
        pl.semaphore_signal(barrier, inc=1, device_id=(me, wrap(ch + o, N_CH)), device_id_type=MESH)
    lax.fori_loop(1, 8, greet([z * 8]), 0)

    loads = [
        pltpu.make_async_copy(src, dst, in_sem.at[i])
        for i, (src, dst) in enumerate(
            [(v_hbm, v_ref), (k_hbm, k_ref), (f_hbm, f_ref), (q_hbm, q_ref), (skip_hbm, skip_row), (w_hbm, w_ref)]
        )
    ]
    table_loads = [
        pltpu.make_async_copy(src, dst, table_sem.at[i])
        for i, (src, dst) in enumerate(
            zip(
                (fa_hbm, fb_hbm, ga_hbm, gb_hbm, ia_hbm, ib_hbm, ja_hbm, jb_hbm, ta_hbm, tb_hbm),
                (fa, fb, ga, gb, ia, ib, ja, jb, ta, tb),
            )
        )
    ]
    for copy in loads + table_loads:
        copy.start()

    def to_chunks(value, send):
        for r in range(ROWS):
            stage[pl.ds(r, N_CTX, stride=ROWS), :] = value(r)
        send[...] = stage[...].astype(BF16).reshape(N_CTX, ROWS, 128)

    def tile(ref, r):
        return ref[:, r * 128 : (r + 1) * 128].astype(F32)

    loads[0].wait()
    loads[1].wait()
    to_chunks(lambda r: tile(v_ref, r) * tile(k_ref, r), send_s)
    loads[2].wait()
    to_chunks(lambda r: tile(f_ref, r), send_f)

    pl.semaphore_wait(barrier, N_CTX - 1 + N_CH - 1)
    def chunk_copy(send, recv, s_sem, r_sem, peer):
        return pltpu.make_async_remote_copy(
            src_ref=send.at[peer], dst_ref=recv.at[me], send_sem=s_sem, recv_sem=r_sem,
            device_id=(peer, ch), device_id_type=MESH,
        )

    def scatter(send, recv, s_sem, r_sem, core):
        for bases in away:

            def step(i, carry, bases=bases):
                to = wrap(lane // 2 + i, 4) * 2 + core
                for base in bases:
                    chunk_copy(send, recv, s_sem, r_sem, base + to).start()
                return carry

            lax.fori_loop(0, 4, step, 0, unroll=2)

        def near(i, carry):
            peer = z * 8 + wrap(lane // 2 + i, 4) * 2 + core

            @pl.when(peer != me)
            def _():
                chunk_copy(send, recv, s_sem, r_sem, peer).start()

            return carry

        lax.fori_loop(0, 4, near, 0)

    def whole(ref, s_sem, r_sem):
        return pltpu.make_async_remote_copy(
            src_ref=ref, dst_ref=ref, send_sem=s_sem, recv_sem=r_sem,
            device_id=(lax.rem(me + 1, N_CTX), ch), device_id_type=MESH,
        )

    def scatter_both(core, carry):
        scatter(send_s, recv_s, s_send, s_recv, core)
        scatter(send_f, recv_f, f_send, f_recv, core)
        return carry

    lax.fori_loop(0, 2, scatter_both, 0)
    pltpu.make_async_copy(send_s.at[me], recv_s.at[me], s_recv).start()
    pltpu.make_async_copy(send_f.at[me], recv_f.at[me], f_recv).start()
    for o in range(1, N_CH):
        pl.semaphore_signal(ready, inc=1, device_id=(me, lax.rem(ch + o, N_CH)), device_id_type=MESH)

    def to_peer(src, dst, s_sem, r_sem, o):
        return pltpu.make_async_remote_copy(
            src_ref=src, dst_ref=dst, send_sem=s_sem, recv_sem=r_sem,
            device_id=(me, lax.rem(ch + o, N_CH)), device_id_type=MESH,
        )

    for copy in loads[3:]:
        copy.wait()
    for y in range(N_CH):
        for i in range(PIECES):
            src = slice(lane_tile(y, i) * 128, lane_tile(y, i) * 128 + 128)
            dst = slice(i * 128, i * 128 + 128)
            side_out[y, 0, :, dst] = q_ref[:, src]
            side_out[y, 1, :, dst] = v_ref[:, src]
    pl.semaphore_wait(ready, N_CH - 1)
    for o in (2, 1, 3):
        to_peer(skip_row, skip_all.at[ch], small_send.at[0], small_recv.at[0], o).start()
        to_peer(w_ref, w_all.at[ch], small_send.at[1], small_recv.at[1], o).start()
        to_peer(side_out.at[lax.rem(ch + o, N_CH)], side_in.at[ch], side_send, side_recv, o).start()
    skip_all[ch] = skip_row[...]
    w_all[ch] = w_ref[...]
    side_in[ch] = side_out[ch]

    for copy in table_loads:
        copy.wait()

    def block(coarse, fine, i):
        ca, sa = coarse[0, pl.ds(i, 1), :], coarse[1, pl.ds(i, 1), :]
        cb, sb = fine[0], fine[1]
        return ca * cb - sa * sb, ca * sb + sa * cb

    def put(high_ref, low_ref, at, value):
        high_ref[at], low_ref[at] = parts_of(value)

    def make_outer(i, carry):
        up = pl.ds(pl.multiple_of(i * 16, 16), 16)
        down = pl.ds(pl.multiple_of(A + i * 16, 16), 16)
        c, s = block(fa, fb, i)
        put(oh, ol, (up,), c)
        put(oh, ol, (down,), -s)
        c, s = block(ga, gb, i)
        put(ph, plo, (up, slice(0, A)), c * (1.0 / T))
        put(ph, plo, (up, slice(A, 2 * A)), s * (-1.0 / T))
        c, s = block(ta, tb, i)
        tc[up, :], ts[up, :] = c, -s
        return carry

    def make_inner(i, carry):
        up = pl.ds(pl.multiple_of(i * 16, 16), 16)
        down = pl.ds(pl.multiple_of(128 + i * 16, 16), 16)
        left, right = slice(0, 128), slice(128, 256)
        for high, low, coarse, fine, sign in ((ah, al, ia, ib, 1.0), (bh, bl, ja, jb, -1.0)):
            c, s = block(coarse, fine, i)
            for k in range(4):
                ck, sk = c[:, k * 128 : k * 128 + 128], s[:, k * 128 : k * 128 + 128]
                put(high, low, (k, up, left), ck)
                put(high, low, (k, down, right), ck)
                put(high, low, (k, up, right), -sign * sk)
                put(high, low, (k, down, left), sign * sk)
        return carry

    lax.fori_loop(0, A // 16, make_outer, 0)
    lax.fori_loop(0, 8, make_inner, 0)

    def load_matrix(recv):
        stage[...] = recv[...].astype(F32).reshape(N_CTX * ROWS, 128)
        for r in range(4):
            x_ref[:, r * 128 : r * 128 + 128] = stage[pl.ds(r, A, stride=4), :].astype(BF16)

    def pair(ref, rows, k, imag):
        return ref[rows, k * 128 : k * 128 + 128], ref[imag, k * 128 : k * 128 + 128]

    def put_pair(k, rows, value):
        for part, at in ((value[0], k * 256), (value[1], k * 256 + 128)):
            s_hi[rows, at : at + 128], s_lo[rows, at : at + 128] = parts_of(part)

    def inner(high, low, k):
        at = slice(k * 256, k * 256 + 256)
        return dot(s_hi[:, at], high[k]) + dot(s_hi[:, at], low[k]) + dot(s_lo[:, at], high[k])

    def forward(recv, out):
        load_matrix(recv)
        z_ref[...] = dot(oh[...], x_ref[...]) + dot(ol[...], x_ref[...])
        for row in range(0, A, TILE):
            rows, imag = slice(row, row + TILE), slice(A + row, A + row + TILE)
            turned = []
            for r in range(4):
                at = slice(r * 128, r * 128 + 128)
                turned.append(mul(pair(z_ref, rows, r, imag), (tc[rows, at], ts[rows, at])))
            for k, value in enumerate(four_point(turned, -1.0)):
                put_pair(k, rows, value)
        for k in range(4):
            out[:, k * 256 : k * 256 + 256] = inner(ah, al, k)

    whole(recv_s, s_send, s_recv).wait_recv()
    forward(recv_s, spec)

    whole(recv_f, f_send, f_recv).wait_recv()
    forward(recv_f, f_spec)
    for k in range(4):
        at, half = slice(k * 256, k * 256 + 128), slice(k * 256 + 128, k * 256 + 256)
        for row in range(0, A, TILE):
            rows = slice(row, row + TILE)
            put_pair(k, rows, mul((spec[rows, at], spec[rows, half]), (f_spec[rows, at], f_spec[rows, half])))
        f_spec[:, k * 256 : k * 256 + 256] = inner(bh, bl, k)
    for row in range(0, A, TILE):
        rows, imag = slice(row, row + TILE), slice(A + row, A + row + TILE)
        back = [
            (f_spec[rows, k * 256 : k * 256 + 128], f_spec[rows, k * 256 + 128 : k * 256 + 256]) for k in range(4)
        ]
        for r, value in enumerate(four_point(back, 1.0)):
            at = slice(r * 128, r * 128 + 128)
            re, im = mul_conj(value, (tc[rows, at], ts[rows, at]))
            y_hi[rows, at], y_lo[rows, at] = parts_of(re)
            y_hi[imag, at], y_lo[imag, at] = parts_of(im)

    sides = [wrap(ch + k, N_CH) for k in range(N_CH)]

    def piece_copy(peer, to):
        return pltpu.make_async_remote_copy(
            src_ref=send_y.at[to, peer], dst_ref=recv_y.at[ch, me], send_sem=y_send, recv_sem=y_recv.at[ch],
            device_id=(peer, to), device_id_type=MESH,
        )

    for part in range(2):
        rows = slice(part * (A // 2), (part + 1) * (A // 2))
        half = slice(part * (N_CTX // 2), (part + 1) * (N_CTX // 2))
        y = dot(ph[rows, :], y_hi[...]) + dot(plo[rows, :], y_hi[...]) + dot(ph[rows, :], y_lo[...])
        for r in range(N_CH):
            send_y[r, half] = y[:, r * 128 : r * 128 + 128].reshape(N_CTX // 2, PIECES, 128).astype(BF16)
        for to_z in ((0, 1, 2, 3), (4, 7, 5, 6))[part]:

            def step(i, carry, base=to_z * 8, part=part, first=int(to_z == 0)):
                peer = base + (wrap(lane + i, 8) if part else wrap(i + first, 8))
                for k in (2, 1, 3):
                    piece_copy(peer, sides[k]).start()

                @pl.when(peer != me)
                def _():
                    piece_copy(peer, ch).start()

                return carry

            lax.fori_loop(0, 8, step, 0, unroll=2)
    pltpu.make_async_copy(send_y.at[ch, me], recv_y.at[ch, me], y_recv.at[ch]).start()

    three = pl.ds(0, N_CH - 1)
    to_peer(skip_all.at[three], skip_all.at[three], small_send.at[0], small_recv.at[0], 1).wait_recv()
    to_peer(w_all.at[three], w_all.at[three], small_send.at[1], small_recv.at[1], 1).wait_recv()
    to_peer(side_in.at[three], side_in.at[three], side_send, side_recv, 1).wait_recv()
    eye = lax.broadcasted_iota(jnp.int32, (N_CTX, N_CTX), 0) == lax.broadcasted_iota(jnp.int32, (N_CTX, N_CTX), 1)
    for y in range(N_CH):
        gain = jnp.sum(jnp.where(eye, skip_all[y], 0.0), axis=1, keepdims=True)
        gain_v[y] = gain * side_in[y, 1].astype(F32)

    for y in range(N_CH):
        whole(recv_y.at[y], y_send, y_recv.at[y]).wait_recv()
        conv32[...] = recv_y[y].astype(F32).reshape(N_CTX * PIECES, 128)
        for i in range(PIECES):
            lanes = slice(i * 128, i * 128 + 128)
            c = conv32[pl.ds(i, N_CTX, stride=PIECES), :]
            value = side_in[y, 0, :, lanes].astype(F32) * (c + gain_v[y, :, lanes])
            gated[y * N_CTX : (y + 1) * N_CTX, lanes] = value.astype(BF16)

    mixed = dot(w_all[...].reshape(N_CH * N_CTX, N_CH * N_CTX), gated[...])
    mix_out[...] = mixed.astype(BF16).reshape(N_CH, N_CTX, PIECES * 128)
    for o in (2, 1, 3):
        to_peer(mix_out.at[lax.rem(ch + o, N_CH)], mix_in.at[ch], mix_send, mix_recv, o).start()
    mix_in[ch] = mix_out[ch]
    to_peer(mix_in.at[three], mix_in.at[three], mix_send, mix_recv, 1).wait_recv()
    for y in range(N_CH):
        for i in range(PIECES):
            at = lane_tile(y, i) * 128
            out_ref[:, at : at + 128] = mix_in[y, :, i * 128 : i * 128 + 128]

    to_peer(skip_all.at[three], skip_all.at[three], small_send.at[0], small_recv.at[0], 1).wait_send()
    to_peer(w_all.at[three], w_all.at[three], small_send.at[1], small_recv.at[1], 1).wait_send()
    to_peer(side_in.at[three], side_in.at[three], side_send, side_recv, 1).wait_send()
    to_peer(mix_in.at[three], mix_in.at[three], mix_send, mix_recv, 1).wait_send()
    most = pl.ds(0, N_CTX - 1)
    whole(send_s.at[most], s_send, s_recv).wait_send()
    whole(send_f.at[most], f_send, f_recv).wait_send()
    whole(send_y.at[three], y_send, y_recv.at[0]).wait_send()
    whole(send_y.at[0, most], y_send, y_recv.at[0]).wait_send()


def on_device(value_in, key_gate, query_gate, filter_taps, skip_gain, out_weight):
    consts = tables()
    args = [value_in, key_gate, query_gate, filter_taps, skip_gain.reshape(1, N_CTX), out_weight.T]
    args += [jnp.asarray(c) for c in consts]
    vm = pltpu.VMEM
    copies = [vm((N_CTX, CHUNK), BF16)] * 3 + [vm((N_CTX, CHUNK), F32), vm((1, N_CTX), F32), vm((N_CTX, N_CH * N_CTX), BF16)]
    copies += [vm((N_CH, 1, N_CTX), F32), vm((N_CH, N_CTX, N_CH * N_CTX), BF16)]
    copies += [vm(c.shape, c.dtype) for c in consts]
    copies += [vm((2 * A, A), BF16)] * 2 + [vm((A, 2 * A), BF16)] * 2 + [vm((4, 256, 256), BF16)] * 4 + [vm((A, B), F32)] * 2
    chunk = vm((N_CTX, ROWS, 128), BF16)
    dma = pltpu.SemaphoreType.DMA
    return pl.pallas_call(
        kernel,
        out_shape=jax.ShapeDtypeStruct((N_CTX, CHUNK), BF16),
        in_specs=[pl.BlockSpec(memory_space=pltpu.HBM)] * len(args),
        out_specs=pl.BlockSpec(memory_space=pltpu.VMEM),
        scratch_shapes=copies
        + [vm((N_CTX * ROWS, 128), F32)]
        + [chunk] * 2
        + [vm((N_CH, N_CTX, PIECES, 128), BF16)]
        + [chunk] * 2
        + [vm((N_CH, N_CTX, PIECES, 128), BF16)]
        + [vm((N_CH, 2, N_CTX, CHUNK // N_CH), BF16)] * 2
        + [
            vm((N_CH, N_CTX, CHUNK // N_CH), F32),
            vm((A, B), BF16),
            vm((2 * A, B), F32),
            vm((A, 2 * B), BF16),
            vm((A, 2 * B), BF16),
            vm((A, 2 * B), F32),
            vm((A, 2 * B), F32),
            vm((2 * A, B), BF16),
            vm((2 * A, B), BF16),
            vm((N_CTX * PIECES, 128), F32),
            vm((N_CH * N_CTX, CHUNK // N_CH), BF16),
            vm((N_CH, N_CTX, CHUNK // N_CH), BF16),
            vm((N_CH, N_CTX, CHUNK // N_CH), BF16),
            dma((6,)), dma((10,)), dma, dma, dma, dma, dma, dma((N_CH,)), dma, dma, dma((2,)), dma((2,)),
            dma, dma, pltpu.SemaphoreType.REGULAR,
        ],
        compiler_params=pltpu.CompilerParams(
            collective_id=0, has_side_effects=True, vmem_limit_bytes=56 * 1024 * 1024
        ),
        name="hyena",
    )(*args)


def solution(mesh):
    placed = (
        P("ch", "ctx"),
        P("ch", "ctx"),
        P("ch", "ctx"),
        P("ch", "ctx"),
        P("ch"),
        P(None, "ch"),
    )
    return jax.shard_map(
        on_device, mesh=mesh, in_specs=placed, out_specs=P("ch", "ctx"), check_vma=False
    )
```

```python
import functools

import jax
import jax.numpy as jnp
import numpy as np
from jax import lax
from jax.experimental import pallas as pl
from jax.experimental.pallas import tpu as pltpu
from jax.sharding import PartitionSpec as P

F32 = jnp.float32
BF16 = jnp.bfloat16
MESH = pl.DeviceIdType.MESH

N_CTX = 64
N_CH = 4
CHUNK = 2048
ROWS = 16
T = N_CTX * CHUNK
A = 256
B = 512
PIECES = ROWS // N_CH
TILE = 32


def turns(rows, columns):
    angle = 2 * np.pi * np.outer(rows, columns)
    return np.stack([np.cos(angle), np.sin(angle)]).astype(np.float32)


@functools.cache
def tables():
    coarse, fine = 16 * np.arange(A // 16), np.arange(16)
    freq, column = np.arange(A) + 0.25, np.arange(B)
    inner = (4 * np.arange(128)[None, :] + np.arange(4)[:, None]).reshape(-1) / B
    lanes = np.tile(np.arange(128), 4)
    back = turns(fine, 4 * lanes / B)
    shift = np.repeat(np.arange(4), 128) * lanes / B
    cs, sn = np.cos(2 * np.pi * shift), np.sin(2 * np.pi * shift)
    back = np.stack([back[0] * cs - back[1] * sn, back[1] * cs + back[0] * sn]).astype(np.float32)
    return (
        turns(coarse, np.arange(A) / A), turns(fine + 0.25, np.arange(A) / A),
        turns(coarse, freq / A), turns(fine, freq / A),
        turns(coarse[:8], inner), turns(fine, inner),
        turns(coarse[:8], 4 * lanes / B), back,
        turns(coarse, column / T), turns(fine + 0.25, column / T),
    )


def dot(a, b):
    return jnp.dot(a, b, preferred_element_type=F32)


def parts_of(x):
    high = x.astype(BF16)
    return high, (x - high.astype(F32)).astype(BF16)


def lane_tile(y, i):
    return 4 * i + y


def mul(a, b):
    return a[0] * b[0] - a[1] * b[1], a[0] * b[1] + a[1] * b[0]


def mul_conj(a, b):
    return a[0] * b[0] + a[1] * b[1], a[1] * b[0] - a[0] * b[1]


def add(a, b):
    return a[0] + b[0], a[1] + b[1]


def sub(a, b):
    return a[0] - b[0], a[1] - b[1]


def four_point(x, sign):
    even, odd = add(x[0], x[2]), add(x[1], x[3])
    even_d, odd_d = sub(x[0], x[2]), sub(x[1], x[3])
    turned = (-sign * odd_d[1], sign * odd_d[0])
    return add(even, odd), add(even_d, turned), sub(even, odd), sub(even_d, turned)


def kernel(
    v_hbm, k_hbm, q_hbm, f_hbm, skip_hbm, w_hbm,
    fa_hbm, fb_hbm, ga_hbm, gb_hbm, ia_hbm, ib_hbm, ja_hbm, jb_hbm, ta_hbm, tb_hbm,
    out_ref,
    v_ref, k_ref, q_ref, f_ref, skip_row, w_ref, skip_all, w_all,
    fa, fb, ga, gb, ia, ib, ja, jb, ta, tb,
    oh, ol, ph, plo, ah, al, bh, bl, tc, ts,
    stage, send_s, send_f, send_y, recv_s, recv_f, recv_y,
    side_out, side_in, gain_v, x_ref, z_ref, s_hi, s_lo, spec, f_spec, y_hi, y_lo, conv32, gated, mix_out, mix_in,
    in_sem, table_sem, s_send, s_recv, f_send, f_recv, y_send, y_recv, side_send, side_recv, small_send, small_recv,
    mix_send, mix_recv, ready,
):
    me = lax.axis_index("ctx")
    ch = lax.axis_index("ch")

    barrier = pltpu.get_barrier_semaphore()

    def wrap(value, size):
        return jnp.where(value >= size, value - size, value)

    z, lane = me // 8, me % 8

    def greet(bases):
        def step(i, carry):
            to = wrap(lane + i, 8)
            for base in bases:
                pl.semaphore_signal(barrier, inc=1, device_id=(base + to, ch), device_id_type=MESH)
            return carry

        return step

    away = [[wrap(z + dz, 8) * 8 for dz in offsets] for offsets in ((4,), (3, 5), (2, 6), (1, 7))]
    for bases in away:
        lax.fori_loop(0, 8, greet(bases), 0, unroll=4)
    for o in range(1, N_CH):
        pl.semaphore_signal(barrier, inc=1, device_id=(me, wrap(ch + o, N_CH)), device_id_type=MESH)
    lax.fori_loop(1, 8, greet([z * 8]), 0)

    loads = [
        pltpu.make_async_copy(src, dst, in_sem.at[i])
        for i, (src, dst) in enumerate(
            [(v_hbm, v_ref), (k_hbm, k_ref), (f_hbm, f_ref), (q_hbm, q_ref), (skip_hbm, skip_row), (w_hbm, w_ref)]
        )
    ]
    table_loads = [
        pltpu.make_async_copy(src, dst, table_sem.at[i])
        for i, (src, dst) in enumerate(
            zip(
                (fa_hbm, fb_hbm, ga_hbm, gb_hbm, ia_hbm, ib_hbm, ja_hbm, jb_hbm, ta_hbm, tb_hbm),
                (fa, fb, ga, gb, ia, ib, ja, jb, ta, tb),
            )
        )
    ]
    for copy in loads + table_loads:
        copy.start()

    def to_chunks(value, send):
        for r in range(ROWS):
            stage[pl.ds(r, N_CTX, stride=ROWS), :] = value(r)
        send[...] = stage[...].astype(BF16).reshape(N_CTX, ROWS, 128)

    def tile(ref, r):
        return ref[:, r * 128 : (r + 1) * 128].astype(F32)

    loads[0].wait()
    loads[1].wait()
    to_chunks(lambda r: tile(v_ref, r) * tile(k_ref, r), send_s)
    loads[2].wait()
    to_chunks(lambda r: tile(f_ref, r), send_f)

    pl.semaphore_wait(barrier, N_CTX - 1 + N_CH - 1)
    def chunk_copy(send, recv, s_sem, r_sem, peer):
        return pltpu.make_async_remote_copy(
            src_ref=send.at[peer], dst_ref=recv.at[me], send_sem=s_sem, recv_sem=r_sem,
            device_id=(peer, ch), device_id_type=MESH,
        )

    def scatter(send, recv, s_sem, r_sem, core):
        for bases in away:

            def step(i, carry, bases=bases):
                to = wrap(lane // 2 + i, 4) * 2 + core
                for base in bases:
                    chunk_copy(send, recv, s_sem, r_sem, base + to).start()
                return carry

            lax.fori_loop(0, 4, step, 0, unroll=2)

        def near(i, carry):
            peer = z * 8 + wrap(lane // 2 + i, 4) * 2 + core

            @pl.when(peer != me)
            def _():
                chunk_copy(send, recv, s_sem, r_sem, peer).start()

            return carry

        lax.fori_loop(0, 4, near, 0)

    def whole(ref, s_sem, r_sem):
        return pltpu.make_async_remote_copy(
            src_ref=ref, dst_ref=ref, send_sem=s_sem, recv_sem=r_sem,
            device_id=(lax.rem(me + 1, N_CTX), ch), device_id_type=MESH,
        )

    def scatter_both(core, carry):
        scatter(send_s, recv_s, s_send, s_recv, core)
        scatter(send_f, recv_f, f_send, f_recv, core)
        return carry

    lax.fori_loop(0, 2, scatter_both, 0)
    pltpu.make_async_copy(send_s.at[me], recv_s.at[me], s_recv).start()
    pltpu.make_async_copy(send_f.at[me], recv_f.at[me], f_recv).start()
    for o in range(1, N_CH):
        pl.semaphore_signal(ready, inc=1, device_id=(me, lax.rem(ch + o, N_CH)), device_id_type=MESH)

    def to_peer(src, dst, s_sem, r_sem, o):
        return pltpu.make_async_remote_copy(
            src_ref=src, dst_ref=dst, send_sem=s_sem, recv_sem=r_sem,
            device_id=(me, lax.rem(ch + o, N_CH)), device_id_type=MESH,
        )

    for copy in loads[3:]:
        copy.wait()
    for y in range(N_CH):
        for i in range(PIECES):
            src = slice(lane_tile(y, i) * 128, lane_tile(y, i) * 128 + 128)
            dst = slice(i * 128, i * 128 + 128)
            side_out[y, 0, :, dst] = q_ref[:, src]
            side_out[y, 1, :, dst] = v_ref[:, src]
    pl.semaphore_wait(ready, N_CH - 1)
    for o in (2, 1, 3):
        to_peer(skip_row, skip_all.at[ch], small_send.at[0], small_recv.at[0], o).start()
        to_peer(w_ref, w_all.at[ch], small_send.at[1], small_recv.at[1], o).start()
        to_peer(side_out.at[lax.rem(ch + o, N_CH)], side_in.at[ch], side_send, side_recv, o).start()
    skip_all[ch] = skip_row[...]
    w_all[ch] = w_ref[...]
    side_in[ch] = side_out[ch]

    for copy in table_loads:
        copy.wait()

    def block(coarse, fine, i):
        ca, sa = coarse[0, pl.ds(i, 1), :], coarse[1, pl.ds(i, 1), :]
        cb, sb = fine[0], fine[1]
        return ca * cb - sa * sb, ca * sb + sa * cb

    def put(high_ref, low_ref, at, value):
        high_ref[at], low_ref[at] = parts_of(value)

    def make_outer(i, carry):
        up = pl.ds(pl.multiple_of(i * 16, 16), 16)
        down = pl.ds(pl.multiple_of(A + i * 16, 16), 16)
        c, s = block(fa, fb, i)
        put(oh, ol, (up,), c)
        put(oh, ol, (down,), -s)
        c, s = block(ga, gb, i)
        put(ph, plo, (up, slice(0, A)), c * (1.0 / T))
        put(ph, plo, (up, slice(A, 2 * A)), s * (-1.0 / T))
        c, s = block(ta, tb, i)
        tc[up, :], ts[up, :] = c, -s
        return carry

    def make_inner(i, carry):
        up = pl.ds(pl.multiple_of(i * 16, 16), 16)
        down = pl.ds(pl.multiple_of(128 + i * 16, 16), 16)
        left, right = slice(0, 128), slice(128, 256)
        for high, low, coarse, fine, sign in ((ah, al, ia, ib, 1.0), (bh, bl, ja, jb, -1.0)):
            c, s = block(coarse, fine, i)
            for k in range(4):
                ck, sk = c[:, k * 128 : k * 128 + 128], s[:, k * 128 : k * 128 + 128]
                put(high, low, (k, up, left), ck)
                put(high, low, (k, down, right), ck)
                put(high, low, (k, up, right), -sign * sk)
                put(high, low, (k, down, left), sign * sk)
        return carry

    lax.fori_loop(0, A // 16, make_outer, 0)
    lax.fori_loop(0, 8, make_inner, 0)

    def load_matrix(recv):
        stage[...] = recv[...].astype(F32).reshape(N_CTX * ROWS, 128)
        for r in range(4):
            x_ref[:, r * 128 : r * 128 + 128] = stage[pl.ds(r, A, stride=4), :].astype(BF16)

    def pair(ref, rows, k, imag):
        return ref[rows, k * 128 : k * 128 + 128], ref[imag, k * 128 : k * 128 + 128]

    def put_pair(k, rows, value):
        for part, at in ((value[0], k * 256), (value[1], k * 256 + 128)):
            s_hi[rows, at : at + 128], s_lo[rows, at : at + 128] = parts_of(part)

    def inner(high, low, k):
        at = slice(k * 256, k * 256 + 256)
        return dot(s_hi[:, at], high[k]) + dot(s_hi[:, at], low[k]) + dot(s_lo[:, at], high[k])

    def forward(recv, out):
        load_matrix(recv)
        z_ref[...] = dot(oh[...], x_ref[...]) + dot(ol[...], x_ref[...])
        for row in range(0, A, TILE):
            rows, imag = slice(row, row + TILE), slice(A + row, A + row + TILE)
            turned = []
            for r in range(4):
                at = slice(r * 128, r * 128 + 128)
                turned.append(mul(pair(z_ref, rows, r, imag), (tc[rows, at], ts[rows, at])))
            for k, value in enumerate(four_point(turned, -1.0)):
                put_pair(k, rows, value)
        for k in range(4):
            out[:, k * 256 : k * 256 + 256] = inner(ah, al, k)

    whole(recv_s, s_send, s_recv).wait_recv()
    forward(recv_s, spec)

    whole(recv_f, f_send, f_recv).wait_recv()
    forward(recv_f, f_spec)
    for k in range(4):
        at, half = slice(k * 256, k * 256 + 128), slice(k * 256 + 128, k * 256 + 256)
        for row in range(0, A, TILE):
            rows = slice(row, row + TILE)
            put_pair(k, rows, mul((spec[rows, at], spec[rows, half]), (f_spec[rows, at], f_spec[rows, half])))
        f_spec[:, k * 256 : k * 256 + 256] = inner(bh, bl, k)
    for row in range(0, A, TILE):
        rows, imag = slice(row, row + TILE), slice(A + row, A + row + TILE)
        back = [
            (f_spec[rows, k * 256 : k * 256 + 128], f_spec[rows, k * 256 + 128 : k * 256 + 256]) for k in range(4)
        ]
        for r, value in enumerate(four_point(back, 1.0)):
            at = slice(r * 128, r * 128 + 128)
            re, im = mul_conj(value, (tc[rows, at], ts[rows, at]))
            y_hi[rows, at], y_lo[rows, at] = parts_of(re)
            y_hi[imag, at], y_lo[imag, at] = parts_of(im)

    sides = [wrap(ch + k, N_CH) for k in range(N_CH)]

    def piece_copy(peer, to):
        return pltpu.make_async_remote_copy(
            src_ref=send_y.at[to, peer], dst_ref=recv_y.at[ch, me], send_sem=y_send, recv_sem=y_recv.at[ch],
            device_id=(peer, to), device_id_type=MESH,
        )

    for part in range(2):
        rows = slice(part * (A // 2), (part + 1) * (A // 2))
        half = slice(part * (N_CTX // 2), (part + 1) * (N_CTX // 2))
        y = dot(ph[rows, :], y_hi[...]) + dot(plo[rows, :], y_hi[...]) + dot(ph[rows, :], y_lo[...])
        for r in range(N_CH):
            send_y[r, half] = y[:, r * 128 : r * 128 + 128].reshape(N_CTX // 2, PIECES, 128).astype(BF16)
        for to_z in ((0, 1, 2, 3), (4, 7, 5, 6))[part]:

            def step(i, carry, base=to_z * 8, part=part, first=int(to_z == 0)):
                peer = base + (wrap(lane + i, 8) if part else wrap(i + first, 8))
                for k in (2, 1, 3):
                    piece_copy(peer, sides[k]).start()

                @pl.when(peer != me)
                def _():
                    piece_copy(peer, ch).start()

                return carry

            lax.fori_loop(0, 8, step, 0, unroll=2)
    pltpu.make_async_copy(send_y.at[ch, me], recv_y.at[ch, me], y_recv.at[ch]).start()

    three = pl.ds(0, N_CH - 1)
    to_peer(skip_all.at[three], skip_all.at[three], small_send.at[0], small_recv.at[0], 1).wait_recv()
    to_peer(w_all.at[three], w_all.at[three], small_send.at[1], small_recv.at[1], 1).wait_recv()
    to_peer(side_in.at[three], side_in.at[three], side_send, side_recv, 1).wait_recv()
    eye = lax.broadcasted_iota(jnp.int32, (N_CTX, N_CTX), 0) == lax.broadcasted_iota(jnp.int32, (N_CTX, N_CTX), 1)
    for y in range(N_CH):
        gain = jnp.sum(jnp.where(eye, skip_all[y], 0.0), axis=1, keepdims=True)
        gain_v[y] = gain * side_in[y, 1].astype(F32)

    for y in range(N_CH):
        whole(recv_y.at[y], y_send, y_recv.at[y]).wait_recv()
        conv32[...] = recv_y[y].astype(F32).reshape(N_CTX * PIECES, 128)
        for i in range(PIECES):
            lanes = slice(i * 128, i * 128 + 128)
            c = conv32[pl.ds(i, N_CTX, stride=PIECES), :]
            value = side_in[y, 0, :, lanes].astype(F32) * (c + gain_v[y, :, lanes])
            gated[y * N_CTX : (y + 1) * N_CTX, lanes] = value.astype(BF16)

    mixed = dot(w_all[...].reshape(N_CH * N_CTX, N_CH * N_CTX), gated[...])
    mix_out[...] = mixed.astype(BF16).reshape(N_CH, N_CTX, PIECES * 128)
    for o in (2, 1, 3):
        to_peer(mix_out.at[lax.rem(ch + o, N_CH)], mix_in.at[ch], mix_send, mix_recv, o).start()
    mix_in[ch] = mix_out[ch]
    to_peer(mix_in.at[three], mix_in.at[three], mix_send, mix_recv, 1).wait_recv()
    for y in range(N_CH):
        for i in range(PIECES):
            at = lane_tile(y, i) * 128
            out_ref[:, at : at + 128] = mix_in[y, :, i * 128 : i * 128 + 128]

    to_peer(skip_all.at[three], skip_all.at[three], small_send.at[0], small_recv.at[0], 1).wait_send()
    to_peer(w_all.at[three], w_all.at[three], small_send.at[1], small_recv.at[1], 1).wait_send()
    to_peer(side_in.at[three], side_in.at[three], side_send, side_recv, 1).wait_send()
    to_peer(mix_in.at[three], mix_in.at[three], mix_send, mix_recv, 1).wait_send()
    most = pl.ds(0, N_CTX - 1)
    whole(send_s.at[most], s_send, s_recv).wait_send()
    whole(send_f.at[most], f_send, f_recv).wait_send()
    whole(send_y.at[three], y_send, y_recv.at[0]).wait_send()
    whole(send_y.at[0, most], y_send, y_recv.at[0]).wait_send()


def on_device(value_in, key_gate, query_gate, filter_taps, skip_gain, out_weight):
    consts = tables()
    args = [value_in, key_gate, query_gate, filter_taps, skip_gain.reshape(1, N_CTX), out_weight.T]
    args += [jnp.asarray(c) for c in consts]
    vm = pltpu.VMEM
    copies = [vm((N_CTX, CHUNK), BF16)] * 3 + [vm((N_CTX, CHUNK), F32), vm((1, N_CTX), F32), vm((N_CTX, N_CH * N_CTX), BF16)]
    copies += [vm((N_CH, 1, N_CTX), F32), vm((N_CH, N_CTX, N_CH * N_CTX), BF16)]
    copies += [vm(c.shape, c.dtype) for c in consts]
    copies += [vm((2 * A, A), BF16)] * 2 + [vm((A, 2 * A), BF16)] * 2 + [vm((4, 256, 256), BF16)] * 4 + [vm((A, B), F32)] * 2
    chunk = vm((N_CTX, ROWS, 128), BF16)
    dma = pltpu.SemaphoreType.DMA
    return pl.pallas_call(
        kernel,
        out_shape=pltpu.VMEM((N_CTX, CHUNK), BF16),
        in_specs=[pl.BlockSpec(memory_space=pltpu.HBM)] * len(args),
        out_specs=pl.BlockSpec(memory_space=pltpu.VMEM),
        scratch_shapes=copies
        + [vm((N_CTX * ROWS, 128), F32)]
        + [chunk] * 2
        + [vm((N_CH, N_CTX, PIECES, 128), BF16)]
        + [chunk] * 2
        + [vm((N_CH, N_CTX, PIECES, 128), BF16)]
        + [vm((N_CH, 2, N_CTX, CHUNK // N_CH), BF16)] * 2
        + [
            vm((N_CH, N_CTX, CHUNK // N_CH), F32),
            vm((A, B), BF16),
            vm((2 * A, B), F32),
            vm((A, 2 * B), BF16),
            vm((A, 2 * B), BF16),
            vm((A, 2 * B), F32),
            vm((A, 2 * B), F32),
            vm((2 * A, B), BF16),
            vm((2 * A, B), BF16),
            vm((N_CTX * PIECES, 128), F32),
            vm((N_CH * N_CTX, CHUNK // N_CH), BF16),
            vm((N_CH, N_CTX, CHUNK // N_CH), BF16),
            vm((N_CH, N_CTX, CHUNK // N_CH), BF16),
            dma((6,)), dma((10,)), dma, dma, dma, dma, dma, dma((N_CH,)), dma, dma, dma((2,)), dma((2,)),
            dma, dma, pltpu.SemaphoreType.REGULAR,
        ],
        compiler_params=pltpu.CompilerParams(
            collective_id=0, has_side_effects=True, vmem_limit_bytes=54 * 1024 * 1024
        ),
        name="hyena",
    )(*args)


def solution(mesh):
    placed = (
        P("ch", "ctx"),
        P("ch", "ctx"),
        P("ch", "ctx"),
        P("ch", "ctx"),
        P("ch"),
        P(None, "ch"),
    )
    return jax.shard_map(
        on_device, mesh=mesh, in_specs=placed, out_specs=P("ch", "ctx"), check_vma=False
    )
```

```python
import functools

import jax
import jax.numpy as jnp
import numpy as np
from jax import lax
from jax.experimental import pallas as pl
from jax.experimental.pallas import tpu as pltpu
from jax.sharding import PartitionSpec as P

F32 = jnp.float32
BF16 = jnp.bfloat16
MESH = pl.DeviceIdType.MESH

N_CTX = 64
N_CH = 4
CHUNK = 2048
ROWS = 16
T = N_CTX * CHUNK
A = 256
B = 512
PIECES = ROWS // N_CH
TILE = 32


def turns(rows, columns):
    angle = 2 * np.pi * np.outer(rows, columns)
    return np.stack([np.cos(angle), np.sin(angle)]).astype(np.float32)


@functools.cache
def tables():
    coarse, fine = 16 * np.arange(A // 16), np.arange(16)
    freq, column = np.arange(A) + 0.25, np.arange(B)
    inner = (4 * np.arange(128)[None, :] + np.arange(4)[:, None]).reshape(-1) / B
    lanes = np.tile(np.arange(128), 4)
    back = turns(fine, 4 * lanes / B)
    shift = np.repeat(np.arange(4), 128) * lanes / B
    cs, sn = np.cos(2 * np.pi * shift), np.sin(2 * np.pi * shift)
    back = np.stack([back[0] * cs - back[1] * sn, back[1] * cs + back[0] * sn]).astype(np.float32)
    return (
        turns(coarse, np.arange(A) / A), turns(fine + 0.25, np.arange(A) / A),
        turns(coarse, freq / A), turns(fine, freq / A),
        turns(coarse[:8], inner), turns(fine, inner),
        turns(coarse[:8], 4 * lanes / B), back,
        turns(coarse, column / T), turns(fine + 0.25, column / T),
    )


def dot(a, b):
    return jnp.dot(a, b, preferred_element_type=F32)


def parts_of(x):
    high = x.astype(BF16)
    return high, (x - high.astype(F32)).astype(BF16)


def lane_tile(y, i):
    return 4 * i + y


def mul(a, b):
    return a[0] * b[0] - a[1] * b[1], a[0] * b[1] + a[1] * b[0]


def mul_conj(a, b):
    return a[0] * b[0] + a[1] * b[1], a[1] * b[0] - a[0] * b[1]


def add(a, b):
    return a[0] + b[0], a[1] + b[1]


def sub(a, b):
    return a[0] - b[0], a[1] - b[1]


def four_point(x, sign):
    even, odd = add(x[0], x[2]), add(x[1], x[3])
    even_d, odd_d = sub(x[0], x[2]), sub(x[1], x[3])
    turned = (-sign * odd_d[1], sign * odd_d[0])
    return add(even, odd), add(even_d, turned), sub(even, odd), sub(even_d, turned)


def kernel(
    v_hbm, k_hbm, q_hbm, f_hbm, skip_hbm, w_hbm,
    fa_hbm, fb_hbm, ga_hbm, gb_hbm, ia_hbm, ib_hbm, ja_hbm, jb_hbm, ta_hbm, tb_hbm,
    out_ref,
    v_ref, k_ref, q_ref, f_ref, skip_row, w_ref, skip_all, w_all,
    fa, fb, ga, gb, ia, ib, ja, jb, ta, tb,
    oh, ol, ph, plo, ah, al, bh, bl, tc, ts,
    stage, send_s, send_f, send_y, recv_s, recv_f, recv_y,
    side_out, side_in, gain_v, x_ref, z_ref, s_hi, s_lo, spec, f_spec, y_hi, y_lo, conv32, gated, mix_out, mix_in,
    in_sem, table_sem, s_send, s_recv, f_send, f_recv, y_send, y_recv, side_send, side_recv, small_send, small_recv,
    mix_send, mix_recv, ready,
):
    me = lax.axis_index("ctx")
    ch = lax.axis_index("ch")

    barrier = pltpu.get_barrier_semaphore()

    def wrap(value, size):
        return jnp.where(value >= size, value - size, value)

    z, lane = me // 8, me % 8

    def greet(bases):
        def step(i, carry):
            to = wrap(lane + i, 8)
            for base in bases:
                pl.semaphore_signal(barrier, inc=1, device_id=(base + to, ch), device_id_type=MESH)
            return carry

        return step

    away = [[wrap(z + dz, 8) * 8 for dz in offsets] for offsets in ((4,), (3, 5), (2, 6), (1, 7))]
    for bases in away:
        lax.fori_loop(0, 8, greet(bases), 0, unroll=4)
    for o in range(1, N_CH):
        pl.semaphore_signal(barrier, inc=1, device_id=(me, wrap(ch + o, N_CH)), device_id_type=MESH)
    lax.fori_loop(1, 8, greet([z * 8]), 0)

    loads = [
        pltpu.make_async_copy(src, dst, in_sem.at[i])
        for i, (src, dst) in enumerate(
            [(v_hbm, v_ref), (k_hbm, k_ref), (f_hbm, f_ref), (q_hbm, q_ref), (skip_hbm, skip_row), (w_hbm, w_ref)]
        )
    ]
    table_loads = [
        pltpu.make_async_copy(src, dst, table_sem.at[i])
        for i, (src, dst) in enumerate(
            zip(
                (fa_hbm, fb_hbm, ga_hbm, gb_hbm, ia_hbm, ib_hbm, ja_hbm, jb_hbm, ta_hbm, tb_hbm),
                (fa, fb, ga, gb, ia, ib, ja, jb, ta, tb),
            )
        )
    ]
    for copy in loads + table_loads:
        copy.start()

    def to_chunks(value, send):
        for r in range(ROWS):
            stage[pl.ds(r, N_CTX, stride=ROWS), :] = value(r)
        send[...] = stage[...].astype(BF16).reshape(N_CTX, ROWS, 128)

    def tile(ref, r):
        return ref[:, r * 128 : (r + 1) * 128].astype(F32)

    loads[0].wait()
    loads[1].wait()
    to_chunks(lambda r: tile(v_ref, r) * tile(k_ref, r), send_s)
    loads[2].wait()
    to_chunks(lambda r: tile(f_ref, r), send_f)

    pl.semaphore_wait(barrier, N_CTX - 1 + N_CH - 1)
    def chunk_copy(send, recv, s_sem, r_sem, peer):
        return pltpu.make_async_remote_copy(
            src_ref=send.at[peer], dst_ref=recv.at[me], send_sem=s_sem, recv_sem=r_sem,
            device_id=(peer, ch), device_id_type=MESH,
        )

    def scatter(send, recv, s_sem, r_sem, core):
        for bases in away:

            def step(i, carry, bases=bases):
                to = wrap(lane // 2 + i, 4) * 2 + core
                for base in bases:
                    chunk_copy(send, recv, s_sem, r_sem, base + to).start()
                return carry

            lax.fori_loop(0, 4, step, 0, unroll=2)

        def near(i, carry):
            peer = z * 8 + wrap(lane // 2 + i, 4) * 2 + core

            @pl.when(peer != me)
            def _():
                chunk_copy(send, recv, s_sem, r_sem, peer).start()

            return carry

        lax.fori_loop(0, 4, near, 0)

    def whole(ref, s_sem, r_sem):
        return pltpu.make_async_remote_copy(
            src_ref=ref, dst_ref=ref, send_sem=s_sem, recv_sem=r_sem,
            device_id=(lax.rem(me + 1, N_CTX), ch), device_id_type=MESH,
        )

    def scatter_both(core, carry):
        scatter(send_s, recv_s, s_send, s_recv, core)
        scatter(send_f, recv_f, f_send, f_recv, core)
        return carry

    lax.fori_loop(0, 2, scatter_both, 0)
    pltpu.make_async_copy(send_s.at[me], recv_s.at[me], s_recv).start()
    pltpu.make_async_copy(send_f.at[me], recv_f.at[me], f_recv).start()
    for o in range(1, N_CH):
        pl.semaphore_signal(ready, inc=1, device_id=(me, lax.rem(ch + o, N_CH)), device_id_type=MESH)

    def to_peer(src, dst, s_sem, r_sem, o):
        return pltpu.make_async_remote_copy(
            src_ref=src, dst_ref=dst, send_sem=s_sem, recv_sem=r_sem,
            device_id=(me, lax.rem(ch + o, N_CH)), device_id_type=MESH,
        )

    for copy in loads[3:]:
        copy.wait()
    for y in range(N_CH):
        for i in range(PIECES):
            src = slice(lane_tile(y, i) * 128, lane_tile(y, i) * 128 + 128)
            dst = slice(i * 128, i * 128 + 128)
            side_out[y, 0, :, dst] = q_ref[:, src]
            side_out[y, 1, :, dst] = v_ref[:, src]
    pl.semaphore_wait(ready, N_CH - 1)
    for o in (2, 1, 3):
        to_peer(skip_row, skip_all.at[ch], small_send.at[0], small_recv.at[0], o).start()
        to_peer(w_ref, w_all.at[ch], small_send.at[1], small_recv.at[1], o).start()
        to_peer(side_out.at[lax.rem(ch + o, N_CH)], side_in.at[ch], side_send, side_recv, o).start()
    skip_all[ch] = skip_row[...]
    w_all[ch] = w_ref[...]
    side_in[ch] = side_out[ch]

    for copy in table_loads:
        copy.wait()

    def block(coarse, fine, i):
        ca, sa = coarse[0, pl.ds(i, 1), :], coarse[1, pl.ds(i, 1), :]
        cb, sb = fine[0], fine[1]
        return ca * cb - sa * sb, ca * sb + sa * cb

    def put(high_ref, low_ref, at, value):
        high_ref[at], low_ref[at] = parts_of(value)

    def make_outer(i, carry):
        up = pl.ds(pl.multiple_of(i * 16, 16), 16)
        down = pl.ds(pl.multiple_of(A + i * 16, 16), 16)
        c, s = block(fa, fb, i)
        put(oh, ol, (up,), c)
        put(oh, ol, (down,), -s)
        c, s = block(ga, gb, i)
        put(ph, plo, (up, slice(0, A)), c * (1.0 / T))
        put(ph, plo, (up, slice(A, 2 * A)), s * (-1.0 / T))
        c, s = block(ta, tb, i)
        tc[up, :], ts[up, :] = c, -s
        return carry

    def make_inner(i, carry):
        up = pl.ds(pl.multiple_of(i * 16, 16), 16)
        down = pl.ds(pl.multiple_of(128 + i * 16, 16), 16)
        left, right = slice(0, 128), slice(128, 256)
        for high, low, coarse, fine, sign in ((ah, al, ia, ib, 1.0), (bh, bl, ja, jb, -1.0)):
            c, s = block(coarse, fine, i)
            for k in range(4):
                ck, sk = c[:, k * 128 : k * 128 + 128], s[:, k * 128 : k * 128 + 128]
                put(high, low, (k, up, left), ck)
                put(high, low, (k, down, right), ck)
                put(high, low, (k, up, right), -sign * sk)
                put(high, low, (k, down, left), sign * sk)
        return carry

    lax.fori_loop(0, A // 16, make_outer, 0)
    lax.fori_loop(0, 8, make_inner, 0)

    def load_matrix(recv):
        stage[...] = recv[...].astype(F32).reshape(N_CTX * ROWS, 128)
        for r in range(4):
            x_ref[:, r * 128 : r * 128 + 128] = stage[pl.ds(r, A, stride=4), :].astype(BF16)

    def pair(ref, rows, k, imag):
        return ref[rows, k * 128 : k * 128 + 128], ref[imag, k * 128 : k * 128 + 128]

    def put_pair(k, rows, value):
        for part, at in ((value[0], k * 256), (value[1], k * 256 + 128)):
            s_hi[rows, at : at + 128], s_lo[rows, at : at + 128] = parts_of(part)

    def inner(high, low, k):
        at = slice(k * 256, k * 256 + 256)
        return dot(s_hi[:, at], high[k]) + dot(s_hi[:, at], low[k]) + dot(s_lo[:, at], high[k])

    def forward(recv, out):
        load_matrix(recv)
        z_ref[...] = dot(oh[...], x_ref[...]) + dot(ol[...], x_ref[...])
        for row in range(0, A, TILE):
            rows, imag = slice(row, row + TILE), slice(A + row, A + row + TILE)
            turned = []
            for r in range(4):
                at = slice(r * 128, r * 128 + 128)
                turned.append(mul(pair(z_ref, rows, r, imag), (tc[rows, at], ts[rows, at])))
            for k, value in enumerate(four_point(turned, -1.0)):
                put_pair(k, rows, value)
        for k in range(4):
            out[:, k * 256 : k * 256 + 256] = inner(ah, al, k)

    whole(recv_s, s_send, s_recv).wait_recv()
    forward(recv_s, spec)

    whole(recv_f, f_send, f_recv).wait_recv()
    forward(recv_f, f_spec)
    for k in range(4):
        at, half = slice(k * 256, k * 256 + 128), slice(k * 256 + 128, k * 256 + 256)
        for row in range(0, A, TILE):
            rows = slice(row, row + TILE)
            put_pair(k, rows, mul((spec[rows, at], spec[rows, half]), (f_spec[rows, at], f_spec[rows, half])))
        f_spec[:, k * 256 : k * 256 + 256] = inner(bh, bl, k)
    for row in range(0, A, TILE):
        rows, imag = slice(row, row + TILE), slice(A + row, A + row + TILE)
        back = [
            (f_spec[rows, k * 256 : k * 256 + 128], f_spec[rows, k * 256 + 128 : k * 256 + 256]) for k in range(4)
        ]
        for r, value in enumerate(four_point(back, 1.0)):
            at = slice(r * 128, r * 128 + 128)
            re, im = mul_conj(value, (tc[rows, at], ts[rows, at]))
            y_hi[rows, at], y_lo[rows, at] = parts_of(re)
            y_hi[imag, at], y_lo[imag, at] = parts_of(im)

    sides = [wrap(ch + k, N_CH) for k in range(N_CH)]

    def piece_copy(peer, to):
        return pltpu.make_async_remote_copy(
            src_ref=send_y.at[to, peer], dst_ref=recv_y.at[ch, me], send_sem=y_send, recv_sem=y_recv.at[ch],
            device_id=(peer, to), device_id_type=MESH,
        )

    for part in range(2):
        rows = slice(part * (A // 2), (part + 1) * (A // 2))
        half = slice(part * (N_CTX // 2), (part + 1) * (N_CTX // 2))
        y = dot(ph[rows, :], y_hi[...]) + dot(plo[rows, :], y_hi[...]) + dot(ph[rows, :], y_lo[...])
        for r in range(N_CH):
            send_y[r, half] = y[:, r * 128 : r * 128 + 128].reshape(N_CTX // 2, PIECES, 128).astype(BF16)
        for to_z in ((0, 1, 2, 3), (4, 7, 5, 6))[part]:

            def step(i, carry, base=to_z * 8, part=part, first=int(to_z == 0)):
                peer = base + (wrap(lane + i, 8) if part else wrap(i + first, 8))
                for k in (2, 1, 3):
                    piece_copy(peer, sides[k]).start()

                @pl.when(peer != me)
                def _():
                    piece_copy(peer, ch).start()

                return carry

            lax.fori_loop(0, 8, step, 0, unroll=4)
    pltpu.make_async_copy(send_y.at[ch, me], recv_y.at[ch, me], y_recv.at[ch]).start()

    three = pl.ds(0, N_CH - 1)
    to_peer(skip_all.at[three], skip_all.at[three], small_send.at[0], small_recv.at[0], 1).wait_recv()
    to_peer(w_all.at[three], w_all.at[three], small_send.at[1], small_recv.at[1], 1).wait_recv()
    to_peer(side_in.at[three], side_in.at[three], side_send, side_recv, 1).wait_recv()
    eye = lax.broadcasted_iota(jnp.int32, (N_CTX, N_CTX), 0) == lax.broadcasted_iota(jnp.int32, (N_CTX, N_CTX), 1)
    for y in range(N_CH):
        gain = jnp.sum(jnp.where(eye, skip_all[y], 0.0), axis=1, keepdims=True)
        gain_v[y] = gain * side_in[y, 1].astype(F32)

    for y in range(N_CH):
        whole(recv_y.at[y], y_send, y_recv.at[y]).wait_recv()
        conv32[...] = recv_y[y].astype(F32).reshape(N_CTX * PIECES, 128)
        for i in range(PIECES):
            lanes = slice(i * 128, i * 128 + 128)
            c = conv32[pl.ds(i, N_CTX, stride=PIECES), :]
            value = side_in[y, 0, :, lanes].astype(F32) * (c + gain_v[y, :, lanes])
            gated[y * N_CTX : (y + 1) * N_CTX, lanes] = value.astype(BF16)

    mixed = dot(w_all[...].reshape(N_CH * N_CTX, N_CH * N_CTX), gated[...])
    mix_out[...] = mixed.astype(BF16).reshape(N_CH, N_CTX, PIECES * 128)
    for o in (2, 1, 3):
        to_peer(mix_out.at[lax.rem(ch + o, N_CH)], mix_in.at[ch], mix_send, mix_recv, o).start()
    mix_in[ch] = mix_out[ch]
    to_peer(mix_in.at[three], mix_in.at[three], mix_send, mix_recv, 1).wait_recv()
    for y in range(N_CH):
        for i in range(PIECES):
            at = lane_tile(y, i) * 128
            out_ref[:, at : at + 128] = mix_in[y, :, i * 128 : i * 128 + 128]

    to_peer(skip_all.at[three], skip_all.at[three], small_send.at[0], small_recv.at[0], 1).wait_send()
    to_peer(w_all.at[three], w_all.at[three], small_send.at[1], small_recv.at[1], 1).wait_send()
    to_peer(side_in.at[three], side_in.at[three], side_send, side_recv, 1).wait_send()
    to_peer(mix_in.at[three], mix_in.at[three], mix_send, mix_recv, 1).wait_send()
    most = pl.ds(0, N_CTX - 1)
    whole(send_s.at[most], s_send, s_recv).wait_send()
    whole(send_f.at[most], f_send, f_recv).wait_send()
    whole(send_y.at[three], y_send, y_recv.at[0]).wait_send()
    whole(send_y.at[0, most], y_send, y_recv.at[0]).wait_send()


def on_device(value_in, key_gate, query_gate, filter_taps, skip_gain, out_weight):
    consts = tables()
    args = [value_in, key_gate, query_gate, filter_taps, skip_gain.reshape(1, N_CTX), out_weight.T]
    args += [jnp.asarray(c) for c in consts]
    vm = pltpu.VMEM
    copies = [vm((N_CTX, CHUNK), BF16)] * 3 + [vm((N_CTX, CHUNK), F32), vm((1, N_CTX), F32), vm((N_CTX, N_CH * N_CTX), BF16)]
    copies += [vm((N_CH, 1, N_CTX), F32), vm((N_CH, N_CTX, N_CH * N_CTX), BF16)]
    copies += [vm(c.shape, c.dtype) for c in consts]
    copies += [vm((2 * A, A), BF16)] * 2 + [vm((A, 2 * A), BF16)] * 2 + [vm((4, 256, 256), BF16)] * 4 + [vm((A, B), F32)] * 2
    chunk = vm((N_CTX, ROWS, 128), BF16)
    dma = pltpu.SemaphoreType.DMA
    return pl.pallas_call(
        kernel,
        out_shape=pltpu.VMEM((N_CTX, CHUNK), BF16),
        in_specs=[pl.BlockSpec(memory_space=pltpu.HBM)] * len(args),
        out_specs=pl.BlockSpec(memory_space=pltpu.VMEM),
        scratch_shapes=copies
        + [vm((N_CTX * ROWS, 128), F32)]
        + [chunk] * 2
        + [vm((N_CH, N_CTX, PIECES, 128), BF16)]
        + [chunk] * 2
        + [vm((N_CH, N_CTX, PIECES, 128), BF16)]
        + [vm((N_CH, 2, N_CTX, CHUNK // N_CH), BF16)] * 2
        + [
            vm((N_CH, N_CTX, CHUNK // N_CH), F32),
            vm((A, B), BF16),
            vm((2 * A, B), F32),
            vm((A, 2 * B), BF16),
            vm((A, 2 * B), BF16),
            vm((A, 2 * B), F32),
            vm((A, 2 * B), F32),
            vm((2 * A, B), BF16),
            vm((2 * A, B), BF16),
            vm((N_CTX * PIECES, 128), F32),
            vm((N_CH * N_CTX, CHUNK // N_CH), BF16),
            vm((N_CH, N_CTX, CHUNK // N_CH), BF16),
            vm((N_CH, N_CTX, CHUNK // N_CH), BF16),
            dma((6,)), dma((10,)), dma, dma, dma, dma, dma, dma((N_CH,)), dma, dma, dma((2,)), dma((2,)),
            dma, dma, pltpu.SemaphoreType.REGULAR,
        ],
        compiler_params=pltpu.CompilerParams(
            collective_id=0, has_side_effects=True, vmem_limit_bytes=54 * 1024 * 1024
        ),
        name="hyena",
    )(*args)


def solution(mesh):
    placed = (
        P("ch", "ctx"),
        P("ch", "ctx"),
        P("ch", "ctx"),
        P("ch", "ctx"),
        P("ch"),
        P(None, "ch"),
    )
    return jax.shard_map(
        on_device, mesh=mesh, in_specs=placed, out_specs=P("ch", "ctx"), check_vma=False
    )
```
